128 devices in a mesh: col: 8 (over z, core), hgt: 16 (over x, y).
Axes of the slice: x: 4, y: 4, z: 4, core: 2. Of those that a mesh axis runs over, the one named last changes fastest.
Arguments:
- efield_lattice_vector: float32 [3, 128, 384, 1024], P(None, 'col', 'hgt'), may hold values from -6 to 6
- hfield_lattice_vector: float32 [3, 128, 384, 1024], P(None, 'col', 'hgt'), may hold values from -6 to 6
- cell_temp: float32 [128, 384, 1024], P('col', 'hgt'), may hold values from -3 to 1
- region_tags: int32 [128, 384, 1024], P('col', 'hgt'), may hold values from 0 to 2
- block_owner: int32 [8, 16, 16, 24, 8, 1], P('col', 'hgt'), may hold values from 0 to 127; in each aligned block of 3072 rows (0 to 3071, 3072 to 6143, ..., all dimensions but the last counted through in order) at most 48 rows name the same one
- block_node: int32 [8, 16, 16, 24, 8], P('col', 'hgt'), may hold values from 0 to 383
- node_enthalpy: float32 [49152, 128], P(('col', 'hgt')), may hold values from -1.5 to 2.5
Outputs:
- e_out: float32 [3, 128, 384, 1024], P(None, 'col', 'hgt')
- h_out: float32 [3, 128, 384, 1024], P(None, 'col', 'hgt')
- node_temp: float32 [49152, 128], P(('col', 'hgt'))
The draws below stay inside these ranges and needn't reach their ends.
Inputs may be any that keep to these rules, and one draw needn't show every extreme that they name: `block_owner`: among the margin blocks of one device, no partition is named by more than 48 blocks, a bound that the blocks of some device reach.
All inputs are finite; a program needn't handle non-finite values.
Results may differ from the reference program's by a relative error of at most 0.0003.
Values sent between devices are 32-bit elements; how exact they have to be, the bound alone decides.
A program may use at most 320 MiB of HBM per device.

```python
import math
import jax
import jax.numpy as jnp
import numpy as np

CX = 16
CZ = 24
NY = 1024
PTS = 128
STEPS = 4
NX = 128
NZ = 384
CAP = 48
NODES = 384
N_COL = 8
N_HGT = 16
DEVICES = 128


def touch_ends(values, key, smallest, top_value):
    extent = values.shape
    index_at = [jax.random.randint(jax.random.fold_in(key, axis), (), 0, extent[axis]) for axis in range(len(extent))]
    values = values.at[tuple(index_at)].set(smallest)
    longest = extent.index(max(extent))
    index_at[longest] = (index_at[longest] + 1) % extent[longest]
    return values.at[tuple(index_at)].set(top_value)


def block_scale(rng, shape, shards, least, high):
    factor_of, own = 1.0, jax.random.fold_in(rng, 6)
    for dim, parts in shards:
        heights = jnp.exp(jax.random.uniform(jax.random.fold_in(own, dim), (parts,), jnp.float32, least / len(shards), high / len(shards)))
        factor_of = factor_of * jnp.repeat(heights, shape[dim] // parts).reshape([-1 if axis == dim else 1 for axis in range(len(shape))])
    return factor_of


def routed_block(own_key, own, number, rows, number_of, top, limit, slope):
    sequence = jax.random.permutation(own_key, number_of)
    packed, usual = portions_of(number_of, rows * top, limit, slope, True), portions_of(number_of, rows * top, limit, slope, False)
    places = jnp.arange(number_of)

    def named(tallies, rotation):
        used = int((tallies > 0).sum())
        fixed = max(1, used // 4)
        moved = fixed + (places - fixed + rotation * (used - fixed)) % max(1, number_of - fixed)
        return jnp.zeros((number_of,), jnp.int32).at[sequence[jnp.where(places < fixed, places, moved)]].set(jnp.asarray(tallies, jnp.int32))

    tallies = jnp.where(number % 4 == 0, named(packed, number // 4), named(usual, number - number // 4 - 1))
    mixed = jax.random.permutation(jax.random.fold_in(own, 3), number_of)
    giver, receiver = mixed[0:number_of // 2 * 2:2], mixed[1:number_of // 2 * 2:2]
    margin = jnp.minimum(tallies[giver] - 1, limit - tallies[receiver]) // 2
    margin = jnp.where((giver == sequence[0]) | (receiver == sequence[0]) | (tallies[receiver] == 0), 0, jnp.maximum(margin, 0))
    moved = jax.random.randint(jax.random.fold_in(own, 4), (number_of // 2,), 0, 1 << 20) % (margin + 1)
    tallies = tallies.at[giver].add(-moved).at[receiver].add(moved)
    labels = jnp.searchsorted(jnp.cumsum(tallies), jnp.arange(rows * top), side="right").astype(jnp.int32)
    grid = labels.reshape(top, rows).T
    grid = grid[jax.random.permutation(jax.random.fold_in(own, 1), rows)]
    rotation = jax.random.randint(jax.random.fold_in(own, 2), (rows, 1), 0, top)
    return jnp.take_along_axis(grid, (jnp.arange(top)[None, :] + rotation) % top, axis=1)


def portions_of(amount, total, reach, slope, full):
    portions = [(1 << 20) // math.isqrt(grade ** slope) + 1 for grade in range(1, amount + 1)]
    largest = reach if full else min(reach, max(-(-total // amount), total * portions[0] // sum(portions)))
    least = 1 if total - largest >= amount - 1 else 0
    holding, rest = [largest] + [least] * (amount - 1), total - largest - least * (amount - 1)
    while rest > 0:
        free = [i for i in range(1, amount) if holding[i] < largest] or [i for i in range(1, amount) if holding[i] < reach]
        whole, left = sum([portions[i] for i in free]), rest
        for i in free:
            more = min(reach - holding[i], max(1, left * portions[i] // whole), rest)
            holding[i] = holding[i] + more
            rest = rest - more
    return np.array(holding)


def centred(stream_key, dims, width, reach, cuts=(), dtype=jnp.bfloat16):
    result = jax.random.normal(stream_key, dims, jnp.float32) * width
    if len(cuts) > 0:
        result = block_scale(stream_key, dims, cuts, -0.22, 0.18) * result
    return jnp.clip(result, min=-reach, max=reach).astype(dtype)


def setup_inputs(seed: int = 0) -> dict:
    key_list = jax.random.split(jax.random.key(seed), 8)
    efield_lattice_vector = centred(key_list[0], (3, NX, NZ, NY), 1.0, 6.0, ((1, 8), (2, 16)), jnp.float32)
    hfield_lattice_vector = centred(key_list[1], (3, NX, NZ, NY), 1.0, 6.0, ((1, 8), (2, 16)), jnp.float32)
    cell_temp = jnp.clip(-3.0 + 4.0 * jax.random.uniform(key_list[2], (NX, NZ, NY), jnp.float32) ** block_scale(key_list[2], (NX, NZ, NY), ((0, 8), (1, 16)), -0.2, 0.2), -3.0, 1.0)
    region_tags = touch_ends(jax.random.randint(key_list[3], (NX, NZ, NY), 0, 3), jax.random.fold_in(key_list[3], 1), 0, 2).astype(jnp.int32)
    block_owner_keys = jax.random.split(jax.random.fold_in(key_list[4], 1), N_COL * N_HGT * CX * CZ * (NY // PTS) // (CX * CZ * (NY // PTS)))
    block_owner_turns = jax.random.permutation(jax.random.fold_in(key_list[4], 3), N_COL * N_HGT * CX * CZ * (NY // PTS) // (CX * CZ * (NY // PTS)))
    block_owner = jax.vmap(lambda own, number: routed_block(jax.random.fold_in(key_list[4], 2), own, number, CX * CZ * (NY // PTS), DEVICES, 1, CAP, 2))(block_owner_keys, block_owner_turns).reshape((N_COL, N_HGT, CX, CZ, NY // PTS, 1))
    block_node = touch_ends(jax.random.randint(key_list[5], (N_COL, N_HGT, CX, CZ, NY // PTS), 0, NODES), jax.random.fold_in(key_list[5], 1), 0, NODES - 1).astype(jnp.int32)
    node_enthalpy = jnp.clip(-1.5 + 4.0 * jax.random.uniform(key_list[6], (DEVICES * NODES, PTS), jnp.float32) ** block_scale(key_list[6], (DEVICES * NODES, PTS), ((0, 128),), -0.2, 0.2), -1.5, 2.5)
    return {"efield_lattice_vector": efield_lattice_vector, "hfield_lattice_vector": hfield_lattice_vector, "cell_temp": cell_temp, "region_tags": region_tags, "block_owner": block_owner, "block_node": block_node, "node_enthalpy": node_enthalpy}


def coefficients(cell_temp, region_tags):
    frac = jax.nn.sigmoid(2.0 * cell_temp)
    lean = region_tags == 0
    fat = region_tags == 1
    eps_frozen = jnp.where(lean, 4.0, jnp.where(fat, 2.5, 5.0))
    eps_thawed = jnp.where(lean, 50.0, jnp.where(fat, 6.0, 10.0))
    sig_frozen = jnp.where(lean, 0.2, jnp.where(fat, 0.05, 0.1))
    melted_conductance = jnp.where(lean, 8.0, jnp.where(fat, 0.4, 1.0))
    eps = eps_frozen + (eps_thawed - eps_frozen) * frac
    sigma = sig_frozen + (melted_conductance - sig_frozen) * frac
    loss = sigma * 0.55 / (2.0 * eps)
    ca = (1.0 - loss) / (1.0 + loss)
    cb = 0.55 / (eps * (1.0 + loss))
    return sigma, ca, cb


def forward(field, plane, axis):
    size = field.shape[axis]
    return jnp.concatenate([jax.lax.slice_in_dim(field, 1, size, axis=axis), plane], axis) - field


def backward(field, plane, axis):
    size = field.shape[axis]
    return field - jnp.concatenate([plane, jax.lax.slice_in_dim(field, 0, size - 1, axis=axis)], axis)


def curl(diff, comps, planes_x, planes_z, plane_y):
    fx, fy, fz = comps
    dx_y = diff(fy, planes_x[0], 0)
    dx_z = diff(fz, planes_x[1], 0)
    dz_x = diff(fx, planes_z[0], 1)
    dz_y = diff(fy, planes_z[1], 1)
    dy_x = diff(fx, plane_y, 2)
    dy_z = diff(fz, plane_y, 2)
    return jnp.stack([dy_z - dz_y, dz_x - dx_z, dx_y - dy_x])


def tissue_warmth_kelvin(heat_content_per_mass):
    return jnp.where(heat_content_per_mass < 0.0, heat_content_per_mass / 2.0, jnp.where(heat_content_per_mass > 1.0, (heat_content_per_mass - 1.0) / 3.0, 0.0))


def reference(efield_lattice_vector, hfield_lattice_vector, cell_temp, region_tags, block_owner, block_node, node_enthalpy):
    sigma, ca, cb = coefficients(cell_temp, region_tags)
    zeros_x = jnp.zeros((2, 1, NZ, NY), jnp.float32)
    zeros_z = jnp.zeros((2, NX, 1, NY), jnp.float32)
    empty_height_plane = jnp.zeros((NX, NZ, 1), jnp.float32)
    power = jnp.zeros((NX, NZ, NY), jnp.float32)
    for step in range(STEPS):
        hfield_lattice_vector = hfield_lattice_vector - 0.55 * curl(forward, (efield_lattice_vector[0], efield_lattice_vector[1], efield_lattice_vector[2]), zeros_x, zeros_z, empty_height_plane)
        efield_lattice_vector = ca * efield_lattice_vector + cb * curl(backward, (hfield_lattice_vector[0], hfield_lattice_vector[1], hfield_lattice_vector[2]), zeros_x, zeros_z, empty_height_plane)
        power = power + sigma * (efield_lattice_vector[0] * efield_lattice_vector[0] + efield_lattice_vector[1] * efield_lattice_vector[1] + efield_lattice_vector[2] * efield_lattice_vector[2])
    absorbed = power / STEPS
    blocks = absorbed.reshape(N_COL, CX, N_HGT, CZ, NY // PTS, PTS).transpose(0, 2, 1, 3, 4, 5).reshape(-1, PTS)
    desired_result = block_owner.reshape(-1) * NODES + block_node.reshape(-1)
    heat = jax.ops.segment_sum(blocks, desired_result, num_segments=DEVICES * NODES)
    heat_content_per_mass = node_enthalpy + 0.25 * heat
    return efield_lattice_vector, hfield_lattice_vector, tissue_warmth_kelvin(heat_content_per_mass)
```

```python
import jax
import jax.numpy as jnp
from jax import lax
from jax.experimental import pallas as pl
from jax.experimental.pallas import tpu as pltpu
from jax.sharding import PartitionSpec as P

STEPS = 4
COURANT = 0.55
MESH = pl.DeviceIdType.MESH
F32 = jnp.float32
ANY = pl.BlockSpec(memory_space=pl.ANY)
HBM = pl.BlockSpec(memory_space=pltpu.HBM)
VMEM = pl.BlockSpec(memory_space=pltpu.VMEM)
SMEM = pl.BlockSpec(memory_space=pltpu.SMEM)


def shifted_up(f):
    axis = f.ndim - 1
    lane = lax.broadcasted_iota(jnp.int32, f.shape, axis)
    sub = lax.broadcasted_iota(jnp.int32, f.shape, axis - 1)
    r = pltpu.roll(f, 127, axis)
    u = pltpu.roll(r, 7, axis - 1)
    return jnp.where(lane < 127, r, jnp.where(sub < 7, u, 0.0))


def shifted_down(f):
    axis = f.ndim - 1
    lane = lax.broadcasted_iota(jnp.int32, f.shape, axis)
    sub = lax.broadcasted_iota(jnp.int32, f.shape, axis - 1)
    r = pltpu.roll(f, 1, axis)
    u = pltpu.roll(r, 1, axis - 1)
    return jnp.where(lane > 0, r, jnp.where(sub > 0, u, 0.0))


def coefficients(temp, tags):
    frac = 1.0 / (1.0 + jnp.exp(-2.0 * temp))
    lean = tags == 0
    fat = tags == 1
    eps_frozen = jnp.where(lean, 4.0, jnp.where(fat, 2.5, 5.0))
    eps_span = jnp.where(lean, 46.0, jnp.where(fat, 3.5, 5.0))
    sig_frozen = jnp.where(lean, 0.2, jnp.where(fat, 0.05, 0.1))
    sig_span = jnp.where(lean, 7.8, jnp.where(fat, 0.35, 0.9))
    eps2 = 2.0 * (eps_frozen + eps_span * frac)
    sigma = sig_frozen + sig_span * frac
    half = sigma * COURANT
    inv = 1.0 / (eps2 + half)
    return sigma, (eps2 - half) * inv, (2.0 * COURANT) * inv


def fields_kernel(nc, nh, e_hbm, h_hbm, t_hbm, g_hbm, e, h, power, tags, sigma, ca, cb, xp, zp, xm, zm, cm, cp,
                  load_sem, ssem, rsem):
    sx, sz = t_hbm.shape[0], t_hbm.shape[1]
    nk = t_hbm.shape[2] // 128
    c = lax.axis_index("col")
    g = lax.axis_index("hgt")
    has_cp, has_cm = c < nc - 1, c > 0
    has_hp, has_hm = g < nh - 1, g > 0

    def lanes(k):
        return pl.ds(k * 128, 128)

    def loads(which):
        out = []
        for k in range(nk):
            if which < 3:
                out.append(pltpu.make_async_copy(
                    e_hbm.at[which, :, :, lanes(k)], e.at[which, pl.ds(0, sx), pl.ds(0, sz), k, :], load_sem.at[which]))
            elif which < 6:
                out.append(pltpu.make_async_copy(
                    h_hbm.at[which - 3, :, :, lanes(k)], h.at[which - 3, pl.ds(1, sx), pl.ds(1, sz), k, :], load_sem.at[which]))
            elif which == 6:
                out.append(pltpu.make_async_copy(t_hbm.at[:, :, lanes(k)], power.at[:, :, k, :], load_sem.at[which]))
            else:
                out.append(pltpu.make_async_copy(g_hbm.at[:, :, lanes(k)], tags.at[:, :, k, :], load_sem.at[which]))
        return out

    all_loads = [loads(w) for w in range(8)]
    for group in all_loads:
        for copy in group:
            copy.start()

    plan = [
        (has_cm, (c - 1, g), has_cp, e.at[pl.ds(1, 2), 0, pl.ds(0, sz)], xp),
        (has_hm, (c, g - 1), has_hp, e.at[pl.ds(0, 2), pl.ds(0, sx), 0], zp),
        (has_cp, (c + 1, g), has_cm, h.at[pl.ds(1, 2), sx, pl.ds(1, sz)], xm),
        (has_hp, (c, g + 1), has_hm, h.at[pl.ds(0, 2), pl.ds(1, sx), sz], zm),
        (has_cp & has_hm, (c + 1, g - 1), has_cm & has_hp, e.at[0, sx - 1, 0], cm),
        (has_cm & has_hp, (c - 1, g + 1), has_cp & has_hm, e.at[2, 0, sz - 1], cp),
    ]

    barrier = pltpu.get_barrier_semaphore()
    for sends, device, _, _, _ in plan:
        @pl.when(sends)
        def _(device=device):
            pl.semaphore_signal(barrier, inc=1, device_id=device, device_id_type=MESH)
    zero_tile = jnp.zeros((8, 128), F32)
    for i in range(3):
        e[i, sx] = jnp.zeros((sz + 1, 8, 128), F32)
        h[i, 0] = jnp.zeros((sz + 1, 8, 128), F32)

    def clear(x, _):
        for i in range(3):
            e[i, x, sz] = zero_tile
            h[i, x + 1, 0] = zero_tile
        return 0

    lax.fori_loop(0, sx, clear, 0)
    peers = 0
    for sends, _, _, _, _ in plan:
        peers = peers + sends.astype(jnp.int32)
    pl.semaphore_wait(barrier, peers)

    def copies(t):
        out = []
        for j, (sends, device, receives, src, buf) in enumerate(plan):
            out.append((sends, receives, pltpu.make_async_remote_copy(
                src_ref=src, dst_ref=buf.at[t], send_sem=ssem.at[t, j], recv_sem=rsem.at[t, j],
                device_id=device, device_id_type=MESH)))
        return out

    def update_h(x, z0, n):
        zs, zn = pl.ds(z0, n), pl.ds(z0 + 1, n)
        ex, ey, ez = e[0, x, zs], e[1, x, zs], e[2, x, zs]
        ex_z, ey_z = e[0, x, zn], e[1, x, zn]
        ey_x, ez_x = e[1, x + 1, zs], e[2, x + 1, zs]
        dy_z = shifted_up(ez) - ez
        dy_x = shifted_up(ex) - ex
        h[0, x + 1, zn] = h[0, x + 1, zn] - COURANT * (dy_z - (ey_z - ey))
        h[1, x + 1, zn] = h[1, x + 1, zn] - COURANT * ((ex_z - ex) - (ez_x - ez))
        h[2, x + 1, zn] = h[2, x + 1, zn] - COURANT * ((ey_x - ey) - dy_x)

    def update_e(x, z0, n):
        zs, zn = pl.ds(z0, n), pl.ds(z0 + 1, n)
        hx, hy, hz = h[0, x + 1, zn], h[1, x + 1, zn], h[2, x + 1, zn]
        hx_z, hy_z = h[0, x + 1, zs], h[1, x + 1, zs]
        hy_x, hz_x = h[1, x, zn], h[2, x, zn]
        dy_z = hz - shifted_down(hz)
        dy_x = hx - shifted_down(hx)
        a, b = ca[x, zs], cb[x, zs]
        ex = a * e[0, x, zs] + b * (dy_z - (hy - hy_z))
        ey = a * e[1, x, zs] + b * ((hx - hx_z) - (hz - hz_x))
        ez = a * e[2, x, zs] + b * ((hy - hy_x) - dy_x)
        e[0, x, zs] = ex
        e[1, x, zs] = ey
        e[2, x, zs] = ez
        power[x, zs] = power[x, zs] + sigma[x, zs] * (ex * ex + ey * ey + ez * ez)

    def over(x_lo, x_hi, z_lo, z_hi, chunk, body):
        count = (z_hi - z_lo) // chunk

        def at(i, _):
            x = x_lo + i // count
            body(x, z_lo + (i % count) * chunk, chunk)
            return 0

        lax.fori_loop(0, (x_hi - x_lo) * count, at, 0)

    def set_coefficients(x, z0, n):
        zs = pl.ds(z0, n)
        s, a, b = coefficients(power[x, zs], tags[x, zs])
        sigma[x, zs] = s
        ca[x, zs] = a
        cb[x, zs] = b
        power[x, zs] = jnp.zeros((n, 8, 128), F32)

    def corrections(t):
        @pl.when(has_cp)
        def _():
            h[1, sx, pl.ds(1, sz)] = h[1, sx, pl.ds(1, sz)] + COURANT * xp[t, 1]
            h[2, sx, pl.ds(1, sz)] = h[2, sx, pl.ds(1, sz)] - COURANT * xp[t, 0]

        @pl.when(has_cm)
        def _():
            h[1, 0, pl.ds(1, sz)] = xm[t, 0] + COURANT * e[2, 0, pl.ds(0, sz)]
            h[2, 0, pl.ds(1, sz)] = xm[t, 1] - COURANT * e[1, 0, pl.ds(0, sz)]

        @pl.when(has_cm & has_hp)
        def _():
            h[1, 0, sz] = h[1, 0, sz] - COURANT * cm[t]

        def rows(x, _):
            @pl.when(has_hp)
            def _():
                h[0, x + 1, sz] = h[0, x + 1, sz] + COURANT * zp[t, 1, x]
                h[1, x + 1, sz] = h[1, x + 1, sz] - COURANT * zp[t, 0, x]

            @pl.when(has_hm)
            def _():
                h[0, x + 1, 0] = zm[t, 0, x] + COURANT * e[1, x, 0]
                h[1, x + 1, 0] = zm[t, 1, x] - COURANT * e[0, x, 0]
            return 0

        lax.fori_loop(0, sx, rows, 0)

        @pl.when(has_cp & has_hm)
        def _():
            h[1, sx, 0] = h[1, sx, 0] + COURANT * cp[t]

    for w in range(6):
        for copy in all_loads[w]:
            copy.wait()
    for t in range(STEPS):
        over(sx - 1, sx, 0, sz, 4, update_h)
        over(0, sx - 1, sz - 1, sz, 1, update_h)
        for sends, _, copy in copies(t):
            pl.when(sends)(copy.start)
        over(0, sx - 1, 0, sz - 2, 2, update_h)
        over(0, sx - 1, sz - 2, sz - 1, 1, update_h)
        if t == 0:
            for w in range(6, 8):
                for copy in all_loads[w]:
                    copy.wait()
            over(0, sx, 0, sz, 4, set_coefficients)
        over(1, sx - 1, 1, sz - 1, 2, update_e)
        for sends, receives, copy in copies(t):
            pl.when(sends)(copy.wait_send)
            pl.when(receives)(copy.wait_recv)
        corrections(t)
        over(0, 1, 0, sz, 2, update_e)
        over(sx - 1, sx, 0, sz, 2, update_e)
        over(1, sx - 1, 0, 1, 1, update_e)
        over(1, sx - 1, sz - 1, sz, 1, update_e)


def route_kernel(n_dev, cap, owner_ref, node_ref, where_ref, nodes_ref):
    rows = owner_ref.shape[0]
    who = lax.broadcasted_iota(jnp.int32, (n_dev, 128), 0)
    earlier = (lax.broadcasted_iota(jnp.int32, (128, 128), 0) < lax.broadcasted_iota(jnp.int32, (128, 128), 1)).astype(jnp.bfloat16)
    slot = lax.broadcasted_iota(jnp.int32, (128, 128), 0)
    base = jnp.zeros((n_dev, 1), F32)
    hi = jnp.zeros((n_dev, 128), F32)
    lo = jnp.zeros((n_dev, 128), F32)
    for r in range(rows):
        own = owner_ref[pl.ds(r, 1), :]
        node = node_ref[pl.ds(r, 1), :] + 1
        hit = who == own
        hit_f = hit.astype(F32)
        hit_b = hit_f.astype(jnp.bfloat16)
        before = jnp.dot(hit_b, earlier, preferred_element_type=F32) + base
        rank = jnp.sum(hit_f * before, axis=0, keepdims=True).astype(jnp.int32)
        base = base + jnp.sum(hit_f, axis=1, keepdims=True)
        where_ref[pl.ds(r, 1), :] = own * cap + rank
        at = slot == rank
        node_hi = (node // 16).astype(F32)
        node_lo = (node % 16).astype(F32)
        dims = (((1,), (1,)), ((), ()))
        hi = hi + lax.dot_general(hit_b, jnp.where(at, node_hi, 0.0).astype(jnp.bfloat16), dims, preferred_element_type=F32)
        lo = lo + lax.dot_general(hit_b, jnp.where(at, node_lo, 0.0).astype(jnp.bfloat16), dims, preferred_element_type=F32)
    nodes_ref[...] = (16.0 * hi + lo).reshape(nodes_ref.shape)


def pack_kernel(where_ref, e, h, power, e_hbm, h_hbm, slots, sem):
    sx, sz = power.shape[0], power.shape[1]
    nk = e_hbm.shape[3] // 128
    copies = []
    for i in range(3):
        for k in range(nk):
            copies.append(pltpu.make_async_copy(
                e.at[i, pl.ds(0, sx), pl.ds(0, sz), k, :], e_hbm.at[i, :, :, pl.ds(k * 128, 128)], sem.at[0]))
            copies.append(pltpu.make_async_copy(
                h.at[i, pl.ds(1, sx), pl.ds(1, sz), k, :], h_hbm.at[i, :, :, pl.ds(k * 128, 128)], sem.at[0]))
    for copy in copies:
        copy.start()
    chunk = 64

    def clear(i, _):
        slots[pl.ds(i * chunk, chunk)] = jnp.zeros((chunk, 1, 128), F32)
        return 0

    lax.fori_loop(0, slots.shape[0] // chunk, clear, 0)

    def place(i, _):
        x, z2 = i // (sz // 2), i % (sz // 2)
        for dz in range(2):
            tile = power[x, z2 * 2 + dz] * (1.0 / STEPS)
            for k in range(nk):
                row = i * 2 * nk + dz * nk + k
                slots[where_ref[row // 128, row % 128]] = tile[k : k + 1, :]
        return 0

    lax.fori_loop(0, sx * sz // 2, place, 0)
    for copy in copies:
        copy.wait()


def deposit_kernel(nc, nh, cap, slots, nodes, enthalpy, out, recv, recv_nodes, ssem, rsem, nsem, msem, lsem):
    n_dev = nc * nh
    c = lax.axis_index("col")
    g = lax.axis_index("hgt")
    me = c * nh + g
    barrier = pltpu.get_barrier_semaphore()

    def partner(d):
        t = me ^ ((d * 37) % n_dev)
        return t, (t // nh, t % nh)

    def greet(d, _):
        pl.semaphore_signal(barrier, inc=1, device_id=partner(d)[1], device_id_type=MESH)
        return 0

    lax.fori_loop(1, n_dev, greet, 0)
    own = pltpu.make_async_copy(slots.at[me], recv.at[me], lsem.at[0])
    own_nodes = pltpu.make_async_copy(nodes.at[me], recv_nodes.at[me], lsem.at[1])
    own.start()
    own_nodes.start()
    pl.semaphore_wait(barrier, n_dev - 1)

    def send(d, _):
        t, device = partner(d)
        pltpu.make_async_remote_copy(nodes.at[t], recv_nodes.at[me], nsem, msem, device_id=device, device_id_type=MESH).start()
        pltpu.make_async_remote_copy(slots.at[t], recv.at[me], ssem, rsem, device_id=device, device_id_type=MESH).start()
        return 0

    lax.fori_loop(1, n_dev, send, 0)
    own.wait()
    own_nodes.wait()
    others = pl.ds(0, n_dev - 1)
    pltpu.make_async_copy(nodes.at[others], recv_nodes.at[others], msem).wait()
    pltpu.make_async_copy(slots.at[others], recv.at[others], rsem).wait()
    n_nodes = enthalpy.shape[0]
    group = 8
    count = lax.broadcasted_iota(jnp.int32, (n_nodes, group * cap), 0).astype(F32) + 1.0

    def add(i, heat):
        rows = recv[pl.ds(i * group, group)].reshape(group * cap, 128)
        high = rows.astype(jnp.bfloat16)
        low = (rows - high.astype(F32)).astype(jnp.bfloat16)
        tags = recv_nodes[pl.ds(i * group, group)]
        tags = jnp.concatenate([tags[s][:, :cap] for s in range(group)], axis=1)
        pick = jnp.where(count == tags, 1.0, 0.0).astype(jnp.bfloat16)
        both = jnp.dot(pick, jnp.concatenate([high, low], axis=1), preferred_element_type=F32)
        return heat + (both[:, :128] + both[:, 128:])

    heat = lax.fori_loop(0, n_dev // group, add, jnp.zeros((n_nodes, 128), F32))
    q = enthalpy[...] + 0.25 * heat
    out[...] = jnp.where(q < 0.0, q / 2.0, jnp.where(q > 1.0, (q - 1.0) / 3.0, 0.0))
    pltpu.make_async_copy(nodes.at[others], recv_nodes.at[others], nsem).wait()
    pltpu.make_async_copy(slots.at[others], recv.at[others], ssem).wait()


def per_device(nc, nh, efield, hfield, cell_temp, region_tags, block_owner, block_node, node_enthalpy):
    sx, sz, sy = cell_temp.shape
    n_dev = nc * nh
    blocks = sx * sz * sy // 128
    cap = 2 * blocks // n_dev
    dma = pltpu.SemaphoreType.DMA

    def tiles(*shape):
        return pltpu.VMEM(shape + (8, 128), F32)

    def out(*shape):
        return jax.ShapeDtypeStruct(shape, F32)

    where_to, nodes = pl.pallas_call(
        lambda *refs: route_kernel(n_dev, cap, *refs),
        out_shape=(jax.ShapeDtypeStruct((blocks // 128, 128), jnp.int32), out(n_dev, 1, 128)),
        in_specs=[VMEM] * 2,
        out_specs=(VMEM, VMEM),
        name="route",
    )(block_owner.reshape(-1, 128), block_node.reshape(-1, 128))
    e, h, power = pl.pallas_call(
        lambda *refs: fields_kernel(nc, nh, *refs),
        out_shape=(tiles(3, sx + 1, sz + 1), tiles(3, sx + 1, sz + 1), tiles(sx, sz)),
        in_specs=[HBM] * 4,
        out_specs=(VMEM, VMEM, VMEM),
        scratch_shapes=[
            pltpu.VMEM((sx, sz, 8, 128), jnp.int32), tiles(sx, sz), tiles(sx, sz), tiles(sx, sz),
            tiles(STEPS, 2, sz), tiles(STEPS, 2, sx), tiles(STEPS, 2, sz), tiles(STEPS, 2, sx), tiles(STEPS), tiles(STEPS),
            dma((8,)), dma((STEPS, 6)), dma((STEPS, 6)),
        ],
        compiler_params=pltpu.CompilerParams(collective_id=0, has_side_effects=True, vmem_limit_bytes=28 << 20),
        name="fields",
    )(efield, hfield, cell_temp, region_tags)
    e_out, h_out, slots = pl.pallas_call(
        pack_kernel,
        out_shape=(out(3, sx, sz, sy), out(3, sx, sz, sy), out(n_dev * cap, 1, 128)),
        in_specs=[SMEM, VMEM, VMEM, VMEM],
        out_specs=(HBM, HBM, VMEM),
        scratch_shapes=[dma((1,))],
        compiler_params=pltpu.CompilerParams(vmem_limit_bytes=24 << 20),
        name="pack",
    )(where_to, e, h, power)
    temp = pl.pallas_call(
        lambda *refs: deposit_kernel(nc, nh, cap, *refs),
        out_shape=out(*node_enthalpy.shape),
        in_specs=[ANY, ANY, VMEM],
        out_specs=VMEM,
        scratch_shapes=[
            pltpu.VMEM((n_dev, cap, 128), F32), pltpu.VMEM((n_dev, 1, 128), F32), dma, dma, dma, dma, dma((2,)),
        ],
        compiler_params=pltpu.CompilerParams(collective_id=1, has_side_effects=True, vmem_limit_bytes=16 << 20),
        name="deposit",
    )(slots.reshape(n_dev, cap, 128), nodes, node_enthalpy)
    return e_out, h_out, temp


def solution(mesh):
    placed = (
        P(None, "col", "hgt", None),
        P(None, "col", "hgt", None),
        P("col", "hgt", None),
        P("col", "hgt", None),
        P("col", "hgt", None, None, None, None),
        P("col", "hgt", None, None, None),
        P(("col", "hgt"), None),
    )
    nc, nh = mesh.shape["col"], mesh.shape["hgt"]
    return jax.shard_map(
        lambda *args: per_device(nc, nh, *args),
        mesh=mesh,
        in_specs=placed,
        out_specs=(P(None, "col", "hgt", None), P(None, "col", "hgt", None), P(("col", "hgt"), None)),
        check_vma=False,
    )
```

```python
import jax
import jax.numpy as jnp
from jax import lax
from jax.experimental import pallas as pl
from jax.experimental.pallas import tpu as pltpu
from jax.sharding import PartitionSpec as P

STEPS = 4
COURANT = 0.55
NXH = 1
NXE = 1
MESH = pl.DeviceIdType.MESH
F32 = jnp.float32
ANY = pl.BlockSpec(memory_space=pl.ANY)
HBM = pl.BlockSpec(memory_space=pltpu.HBM)
VMEM = pl.BlockSpec(memory_space=pltpu.VMEM)
SMEM = pl.BlockSpec(memory_space=pltpu.SMEM)


def shifted_up(f):
    axis = f.ndim - 1
    lane = lax.broadcasted_iota(jnp.int32, f.shape, axis)
    sub = lax.broadcasted_iota(jnp.int32, f.shape, axis - 1)
    r = pltpu.roll(f, 127, axis)
    u = pltpu.roll(r, 7, axis - 1)
    return jnp.where(lane < 127, r, jnp.where(sub < 7, u, 0.0))


def shifted_down(f):
    axis = f.ndim - 1
    lane = lax.broadcasted_iota(jnp.int32, f.shape, axis)
    sub = lax.broadcasted_iota(jnp.int32, f.shape, axis - 1)
    r = pltpu.roll(f, 1, axis)
    u = pltpu.roll(r, 1, axis - 1)
    return jnp.where(lane > 0, r, jnp.where(sub > 0, u, 0.0))


def coefficients(temp, tags):
    frac = 1.0 / (1.0 + jnp.exp(-2.0 * temp))
    lean = tags == 0
    fat = tags == 1
    eps_frozen = jnp.where(lean, 4.0, jnp.where(fat, 2.5, 5.0))
    eps_span = jnp.where(lean, 46.0, jnp.where(fat, 3.5, 5.0))
    sig_frozen = jnp.where(lean, 0.2, jnp.where(fat, 0.05, 0.1))
    sig_span = jnp.where(lean, 7.8, jnp.where(fat, 0.35, 0.9))
    eps2 = 2.0 * (eps_frozen + eps_span * frac)
    sigma = sig_frozen + sig_span * frac
    half = sigma * COURANT
    inv = 1.0 / (eps2 + half)
    return sigma, (eps2 - half) * inv, (2.0 * COURANT) * inv


def fields_kernel(nc, nh, e_hbm, h_hbm, t_hbm, g_hbm, e, h, power, tags, sigma, ca, cb, xp, zp, xm, zm, cm, cp,
                  load_sem, ssem, rsem):
    sx, sz = t_hbm.shape[0], t_hbm.shape[1]
    nk = t_hbm.shape[2] // 128
    c = lax.axis_index("col")
    g = lax.axis_index("hgt")
    has_cp, has_cm = c < nc - 1, c > 0
    has_hp, has_hm = g < nh - 1, g > 0

    def lanes(k):
        return pl.ds(k * 128, 128)

    def loads(which):
        out = []
        for k in range(nk):
            if which < 3:
                out.append(pltpu.make_async_copy(
                    e_hbm.at[which, :, :, lanes(k)], e.at[which, pl.ds(0, sx), pl.ds(0, sz), k, :], load_sem.at[which]))
            elif which < 6:
                out.append(pltpu.make_async_copy(
                    h_hbm.at[which - 3, :, :, lanes(k)], h.at[which - 3, pl.ds(1, sx), pl.ds(1, sz), k, :], load_sem.at[which]))
            elif which == 6:
                out.append(pltpu.make_async_copy(t_hbm.at[:, :, lanes(k)], power.at[:, :, k, :], load_sem.at[which]))
            else:
                out.append(pltpu.make_async_copy(g_hbm.at[:, :, lanes(k)], tags.at[:, :, k, :], load_sem.at[which]))
        return out

    all_loads = [loads(w) for w in range(8)]
    for group in all_loads:
        for copy in group:
            copy.start()

    plan = [
        (has_cm, (c - 1, g), has_cp, e.at[pl.ds(1, 2), 0, pl.ds(0, sz)], xp),
        (has_hm, (c, g - 1), has_hp, e.at[pl.ds(0, 2), pl.ds(0, sx), 0], zp),
        (has_cp, (c + 1, g), has_cm, h.at[pl.ds(1, 2), sx, pl.ds(1, sz)], xm),
        (has_hp, (c, g + 1), has_hm, h.at[pl.ds(0, 2), pl.ds(1, sx), sz], zm),
        (has_cp & has_hm, (c + 1, g - 1), has_cm & has_hp, e.at[0, sx - 1, 0], cm),
        (has_cm & has_hp, (c - 1, g + 1), has_cp & has_hm, e.at[2, 0, sz - 1], cp),
    ]

    barrier = pltpu.get_barrier_semaphore()
    for sends, device, _, _, _ in plan:
        @pl.when(sends)
        def _(device=device):
            pl.semaphore_signal(barrier, inc=1, device_id=device, device_id_type=MESH)
    zero_tile = jnp.zeros((8, 128), F32)
    for i in range(3):
        e[i, sx] = jnp.zeros((sz + 1, 8, 128), F32)
        h[i, 0] = jnp.zeros((sz + 1, 8, 128), F32)

    def clear(x, _):
        for i in range(3):
            e[i, x, sz] = zero_tile
            h[i, x + 1, 0] = zero_tile
        return 0

    lax.fori_loop(0, sx, clear, 0)
    peers = 0
    for sends, _, _, _, _ in plan:
        peers = peers + sends.astype(jnp.int32)
    pl.semaphore_wait(barrier, peers)

    def copies(t):
        out = []
        for j, (sends, device, receives, src, buf) in enumerate(plan):
            out.append((sends, receives, pltpu.make_async_remote_copy(
                src_ref=src, dst_ref=buf.at[t], send_sem=ssem.at[t, j], recv_sem=rsem.at[t, j],
                device_id=device, device_id_type=MESH)))
        return out

    def update_h(x, nx, z0, nz):
        xs, xn, zs, zn, zw = pl.ds(x, nx), pl.ds(x + 1, nx), pl.ds(z0, nz), pl.ds(z0 + 1, nz), pl.ds(z0, nz + 1)
        ex, ey, ez = e[0, xs, zw], e[1, xs, zw], e[2, xs, zs]
        ey_x, ez_x = e[1, xn, zs], e[2, xn, zs]
        hx, hy, hz = h[0, xn, zn], h[1, xn, zn], h[2, xn, zn]
        ex, ex_z = ex[:, :nz], ex[:, 1:]
        ey, ey_z = ey[:, :nz], ey[:, 1:]
        hx = hx - COURANT * ((shifted_up(ez) - ez) - (ey_z - ey))
        hy = hy - COURANT * ((ex_z - ex) - (ez_x - ez))
        hz = hz - COURANT * ((ey_x - ey) - (shifted_up(ex) - ex))
        h[0, xn, zn] = hx
        h[1, xn, zn] = hy
        h[2, xn, zn] = hz

    def update_e(x, nx, z0, nz):
        xs, xn, zs, zn, zw = pl.ds(x, nx), pl.ds(x + 1, nx), pl.ds(z0, nz), pl.ds(z0 + 1, nz), pl.ds(z0, nz + 1)
        hx, hy, hz = h[0, xn, zw], h[1, xn, zw], h[2, xn, zn]
        hy_x, hz_x = h[1, xs, zn], h[2, xs, zn]
        ex, ey, ez = e[0, xs, zs], e[1, xs, zs], e[2, xs, zs]
        a, b, s, p = ca[xs, zs], cb[xs, zs], sigma[xs, zs], power[xs, zs]
        hx_z, hx = hx[:, :nz], hx[:, 1:]
        hy_z, hy = hy[:, :nz], hy[:, 1:]
        ex = a * ex + b * ((hz - shifted_down(hz)) - (hy - hy_z))
        ey = a * ey + b * ((hx - hx_z) - (hz - hz_x))
        ez = a * ez + b * ((hy - hy_x) - (hx - shifted_down(hx)))
        e[0, xs, zs] = ex
        e[1, xs, zs] = ey
        e[2, xs, zs] = ez
        power[xs, zs] = p + s * (ex * ex + ey * ey + ez * ez)

    def over(x_lo, x_hi, nx, z_lo, z_hi, body):
        def at(i, _):
            body(x_lo + i * nx, nx, z_lo, z_hi - z_lo)
            return 0

        lax.fori_loop(0, (x_hi - x_lo) // nx, at, 0)

    def set_coefficients(x, nx, z0, nz):
        xs, zs = pl.ds(x, nx), pl.ds(z0, nz)
        s, a, b = coefficients(power[xs, zs], tags[xs, zs])
        sigma[xs, zs] = s
        ca[xs, zs] = a
        cb[xs, zs] = b
        power[xs, zs] = jnp.zeros((nx, nz, 8, 128), F32)

    def corrections(t):
        @pl.when(has_cp)
        def _():
            h[1, sx, pl.ds(1, sz)] = h[1, sx, pl.ds(1, sz)] + COURANT * xp[t, 1]
            h[2, sx, pl.ds(1, sz)] = h[2, sx, pl.ds(1, sz)] - COURANT * xp[t, 0]

        @pl.when(has_cm)
        def _():
            h[1, 0, pl.ds(1, sz)] = xm[t, 0] + COURANT * e[2, 0, pl.ds(0, sz)]
            h[2, 0, pl.ds(1, sz)] = xm[t, 1] - COURANT * e[1, 0, pl.ds(0, sz)]

        @pl.when(has_cm & has_hp)
        def _():
            h[1, 0, sz] = h[1, 0, sz] - COURANT * cm[t]

        def rows(x, _):
            @pl.when(has_hp)
            def _():
                h[0, x + 1, sz] = h[0, x + 1, sz] + COURANT * zp[t, 1, x]
                h[1, x + 1, sz] = h[1, x + 1, sz] - COURANT * zp[t, 0, x]

            @pl.when(has_hm)
            def _():
                h[0, x + 1, 0] = zm[t, 0, x] + COURANT * e[1, x, 0]
                h[1, x + 1, 0] = zm[t, 1, x] - COURANT * e[0, x, 0]
            return 0

        lax.fori_loop(0, sx, rows, 0)

        @pl.when(has_cp & has_hm)
        def _():
            h[1, sx, 0] = h[1, sx, 0] + COURANT * cp[t]

    for w in range(6):
        for copy in all_loads[w]:
            copy.wait()
    for t in range(STEPS):
        update_h(sx - 1, 1, 0, sz)
        update_h(0, sx - 1, sz - 1, 1)
        for sends, _, copy in copies(t):
            pl.when(sends)(copy.start)
        over(0, sx - 1, NXH, 0, sz - 1, update_h)
        if t == 0:
            for w in range(6, 8):
                for copy in all_loads[w]:
                    copy.wait()
            over(0, sx, 1, 0, sz, set_coefficients)
        over(1, sx - 1, NXE, 1, sz - 1, update_e)
        for sends, receives, copy in copies(t):
            pl.when(sends)(copy.wait_send)
            pl.when(receives)(copy.wait_recv)
        corrections(t)
        update_e(0, 1, 0, sz)
        update_e(sx - 1, 1, 0, sz)
        update_e(1, sx - 2, 0, 1)
        update_e(1, sx - 2, sz - 1, 1)


def route_kernel(n_dev, cap, owner_ref, node_ref, where_ref, nodes_ref):
    rows = owner_ref.shape[0]
    who = lax.broadcasted_iota(jnp.int32, (n_dev, 128), 0)
    earlier = (lax.broadcasted_iota(jnp.int32, (128, 128), 0) < lax.broadcasted_iota(jnp.int32, (128, 128), 1)).astype(jnp.bfloat16)
    slot = lax.broadcasted_iota(jnp.int32, (128, 128), 0)
    base = jnp.zeros((n_dev, 1), F32)
    hi = jnp.zeros((n_dev, 128), F32)
    lo = jnp.zeros((n_dev, 128), F32)
    for r in range(rows):
        own = owner_ref[pl.ds(r, 1), :]
        node = node_ref[pl.ds(r, 1), :] + 1
        hit = who == own
        hit_f = hit.astype(F32)
        hit_b = hit_f.astype(jnp.bfloat16)
        before = jnp.dot(hit_b, earlier, preferred_element_type=F32) + base
        rank = jnp.sum(hit_f * before, axis=0, keepdims=True).astype(jnp.int32)
        base = base + jnp.sum(hit_f, axis=1, keepdims=True)
        where_ref[pl.ds(r, 1), :] = own * cap + rank
        at = slot == rank
        node_hi = (node // 16).astype(F32)
        node_lo = (node % 16).astype(F32)
        dims = (((1,), (1,)), ((), ()))
        hi = hi + lax.dot_general(hit_b, jnp.where(at, node_hi, 0.0).astype(jnp.bfloat16), dims, preferred_element_type=F32)
        lo = lo + lax.dot_general(hit_b, jnp.where(at, node_lo, 0.0).astype(jnp.bfloat16), dims, preferred_element_type=F32)
    nodes_ref[...] = (16.0 * hi + lo).reshape(nodes_ref.shape)


def pack_kernel(where_ref, e, h, power, e_hbm, h_hbm, slots, sem):
    sx, sz = e_hbm.shape[1], e_hbm.shape[2]
    nk = e_hbm.shape[3] // 128
    copies = []
    for i in range(3):
        for k in range(nk):
            copies.append(pltpu.make_async_copy(
                e.at[i, pl.ds(0, sx), pl.ds(0, sz), k, :], e_hbm.at[i, :, :, pl.ds(k * 128, 128)], sem.at[0]))
            copies.append(pltpu.make_async_copy(
                h.at[i, pl.ds(1, sx), pl.ds(1, sz), k, :], h_hbm.at[i, :, :, pl.ds(k * 128, 128)], sem.at[0]))
    for copy in copies:
        copy.start()
    chunk = 64

    def clear(i, _):
        slots[pl.ds(i * chunk, chunk)] = jnp.zeros((chunk, 1, 128), F32)
        return 0

    lax.fori_loop(0, slots.shape[0] // chunk, clear, 0)

    tiles = where_ref.shape[1] // nk

    def place(i, _):
        for j in range(tiles):
            tile = power[i * tiles + j] * (1.0 / STEPS)
            for k in range(nk):
                slots[where_ref[i, j * nk + k]] = tile[k : k + 1, :]
        return 0

    lax.fori_loop(0, where_ref.shape[0], place, 0)
    for copy in copies:
        copy.wait()


def deposit_kernel(nc, nh, cap, slots, nodes, enthalpy, out, recv, recv_nodes, ssem, rsem, nsem, msem, lsem):
    n_dev = nc * nh
    c = lax.axis_index("col")
    g = lax.axis_index("hgt")
    me = c * nh + g
    barrier = pltpu.get_barrier_semaphore()

    def partner(d):
        t = me ^ ((d * 37) % n_dev)
        return t, (t // nh, t % nh)

    def greet(d, _):
        pl.semaphore_signal(barrier, inc=1, device_id=partner(d)[1], device_id_type=MESH)
        return 0

    lax.fori_loop(1, n_dev, greet, 0)
    own = pltpu.make_async_copy(slots.at[me], recv.at[me], lsem.at[0])
    own_nodes = pltpu.make_async_copy(nodes.at[me], recv_nodes.at[me], lsem.at[1])
    own.start()
    own_nodes.start()
    pl.semaphore_wait(barrier, n_dev - 1)

    def send(d, _):
        t, device = partner(d)
        pltpu.make_async_remote_copy(nodes.at[t], recv_nodes.at[me], nsem, msem, device_id=device, device_id_type=MESH).start()
        pltpu.make_async_remote_copy(slots.at[t], recv.at[me], ssem, rsem, device_id=device, device_id_type=MESH).start()
        return 0

    lax.fori_loop(1, n_dev, send, 0)
    own.wait()
    own_nodes.wait()
    others = pl.ds(0, n_dev - 1)
    pltpu.make_async_copy(nodes.at[others], recv_nodes.at[others], msem).wait()
    pltpu.make_async_copy(slots.at[others], recv.at[others], rsem).wait()
    n_nodes = enthalpy.shape[0]
    group = 8
    count = lax.broadcasted_iota(jnp.int32, (n_nodes, group * cap), 0).astype(F32) + 1.0

    def add(i, heat):
        rows = recv[pl.ds(i * group, group)].reshape(group * cap, 128)
        high = rows.astype(jnp.bfloat16)
        low = (rows - high.astype(F32)).astype(jnp.bfloat16)
        tags = recv_nodes[pl.ds(i * group, group)]
        tags = jnp.concatenate([tags[s][:, :cap] for s in range(group)], axis=1)
        pick = jnp.where(count == tags, 1.0, 0.0).astype(jnp.bfloat16)
        both = jnp.dot(pick, jnp.concatenate([high, low], axis=1), preferred_element_type=F32)
        return heat + (both[:, :128] + both[:, 128:])

    heat = lax.fori_loop(0, n_dev // group, add, jnp.zeros((n_nodes, 128), F32))
    q = enthalpy[...] + 0.25 * heat
    out[...] = jnp.where(q < 0.0, q / 2.0, jnp.where(q > 1.0, (q - 1.0) / 3.0, 0.0))
    pltpu.make_async_copy(nodes.at[others], recv_nodes.at[others], nsem).wait()
    pltpu.make_async_copy(slots.at[others], recv.at[others], ssem).wait()


def per_device(nc, nh, efield, hfield, cell_temp, region_tags, block_owner, block_node, node_enthalpy):
    sx, sz, sy = cell_temp.shape
    n_dev = nc * nh
    blocks = sx * sz * sy // 128
    cap = 2 * blocks // n_dev
    dma = pltpu.SemaphoreType.DMA

    def tiles(*shape):
        return pltpu.VMEM(shape + (8, 128), F32)

    def out(*shape):
        return jax.ShapeDtypeStruct(shape, F32)

    where_to, nodes = pl.pallas_call(
        lambda *refs: route_kernel(n_dev, cap, *refs),
        out_shape=(jax.ShapeDtypeStruct((blocks // 128, 128), jnp.int32), out(n_dev, 1, 128)),
        in_specs=[VMEM] * 2,
        out_specs=(VMEM, VMEM),
        name="route",
    )(block_owner.reshape(-1, 128), block_node.reshape(-1, 128))
    e, h, power = pl.pallas_call(
        lambda *refs: fields_kernel(nc, nh, *refs),
        out_shape=(tiles(3, sx + 1, sz + 1), tiles(3, sx + 1, sz + 1), tiles(sx, sz)),
        in_specs=[HBM] * 4,
        out_specs=(VMEM, VMEM, VMEM),
        scratch_shapes=[
            pltpu.VMEM((sx, sz, 8, 128), jnp.int32), tiles(sx, sz), tiles(sx, sz), tiles(sx, sz),
            tiles(STEPS, 2, sz), tiles(STEPS, 2, sx), tiles(STEPS, 2, sz), tiles(STEPS, 2, sx), tiles(STEPS), tiles(STEPS),
            dma((8,)), dma((STEPS, 6)), dma((STEPS, 6)),
        ],
        compiler_params=pltpu.CompilerParams(collective_id=0, has_side_effects=True, vmem_limit_bytes=48 << 20),
        name="fields",
    )(efield, hfield, cell_temp, region_tags)
    e_out, h_out, slots = pl.pallas_call(
        pack_kernel,
        out_shape=(out(3, sx, sz, sy), out(3, sx, sz, sy), out(n_dev * cap, 1, 128)),
        in_specs=[SMEM, VMEM, VMEM, VMEM],
        out_specs=(HBM, HBM, VMEM),
        scratch_shapes=[dma((1,))],
        compiler_params=pltpu.CompilerParams(vmem_limit_bytes=24 << 20),
        name="pack",
    )(where_to, e, h, power.reshape(sx * sz, 8, 128))
    temp = pl.pallas_call(
        lambda *refs: deposit_kernel(nc, nh, cap, *refs),
        out_shape=out(*node_enthalpy.shape),
        in_specs=[ANY, ANY, VMEM],
        out_specs=VMEM,
        scratch_shapes=[
            pltpu.VMEM((n_dev, cap, 128), F32), pltpu.VMEM((n_dev, 1, 128), F32), dma, dma, dma, dma, dma((2,)),
        ],
        compiler_params=pltpu.CompilerParams(collective_id=1, has_side_effects=True, vmem_limit_bytes=16 << 20),
        name="deposit",
    )(slots.reshape(n_dev, cap, 128), nodes, node_enthalpy)
    return e_out, h_out, temp


def solution(mesh):
    placed = (
        P(None, "col", "hgt", None),
        P(None, "col", "hgt", None),
        P("col", "hgt", None),
        P("col", "hgt", None),
        P("col", "hgt", None, None, None, None),
        P("col", "hgt", None, None, None),
        P(("col", "hgt"), None),
    )
    nc, nh = mesh.shape["col"], mesh.shape["hgt"]
    return jax.shard_map(
        lambda *args: per_device(nc, nh, *args),
        mesh=mesh,
        in_specs=placed,
        out_specs=(P(None, "col", "hgt", None), P(None, "col", "hgt", None), P(("col", "hgt"), None)),
        check_vma=False,
    )
```

```python
import jax
import jax.numpy as jnp
from jax import lax
from jax.experimental import pallas as pl
from jax.experimental.pallas import tpu as pltpu
from jax.sharding import PartitionSpec as P

STEPS = 4
COURANT = 0.55
NXH = 1
NXE = 1
GROUP = 8
MESH = pl.DeviceIdType.MESH
F32 = jnp.float32
HBM = pl.BlockSpec(memory_space=pltpu.HBM)
VMEM = pl.BlockSpec(memory_space=pltpu.VMEM)
SMEM = pl.BlockSpec(memory_space=pltpu.SMEM)


def shifted_up(f):
    axis = f.ndim - 1
    lane = lax.broadcasted_iota(jnp.int32, f.shape, axis)
    sub = lax.broadcasted_iota(jnp.int32, f.shape, axis - 1)
    r = pltpu.roll(f, 127, axis)
    u = pltpu.roll(r, 7, axis - 1)
    return jnp.where(lane < 127, r, jnp.where(sub < 7, u, 0.0))


def shifted_down(f):
    axis = f.ndim - 1
    lane = lax.broadcasted_iota(jnp.int32, f.shape, axis)
    sub = lax.broadcasted_iota(jnp.int32, f.shape, axis - 1)
    r = pltpu.roll(f, 1, axis)
    u = pltpu.roll(r, 1, axis - 1)
    return jnp.where(lane > 0, r, jnp.where(sub > 0, u, 0.0))


def coefficients(temp, tags):
    frac = 1.0 / (1.0 + jnp.exp(-2.0 * temp))
    lean = tags == 0
    fat = tags == 1
    eps_frozen = jnp.where(lean, 4.0, jnp.where(fat, 2.5, 5.0))
    eps_span = jnp.where(lean, 46.0, jnp.where(fat, 3.5, 5.0))
    sig_frozen = jnp.where(lean, 0.2, jnp.where(fat, 0.05, 0.1))
    sig_span = jnp.where(lean, 7.8, jnp.where(fat, 0.35, 0.9))
    eps2 = 2.0 * (eps_frozen + eps_span * frac)
    sigma = sig_frozen + sig_span * frac
    half = sigma * COURANT
    inv = 1.0 / (eps2 + half)
    return sigma, (eps2 - half) * inv, (2.0 * COURANT) * inv


def fields_kernel(nc, nh, cap, source, e_hbm, h_hbm, t_hbm, g_hbm, nodes, enthalpy, e, h, out,
                  power, tags, sigma, ca, cb, xp, zp, xm, zm, cm, cp, send, recv, recv_nodes,
                  load_sem, ssem, rsem, ready, local_sem, out_sem, in_sem, node_out_sem, node_in_sem):
    n_dev = nc * nh
    sx, sz = t_hbm.shape[0], t_hbm.shape[1]
    nk = t_hbm.shape[2] // 128
    c = lax.axis_index("col")
    g = lax.axis_index("hgt")
    has_cp, has_cm = c < nc - 1, c > 0
    has_hp, has_hm = g < nh - 1, g > 0

    def lanes(k):
        return pl.ds(k * 128, 128)

    def loads(which):
        out = []
        for k in range(nk):
            if which < 3:
                out.append(pltpu.make_async_copy(
                    e_hbm.at[which, :, :, lanes(k)], e.at[which, pl.ds(0, sx), pl.ds(0, sz), k, :], load_sem.at[which]))
            elif which < 6:
                out.append(pltpu.make_async_copy(
                    h_hbm.at[which - 3, :, :, lanes(k)], h.at[which - 3, pl.ds(1, sx), pl.ds(1, sz), k, :], load_sem.at[which]))
            elif which == 6:
                out.append(pltpu.make_async_copy(t_hbm.at[:, :, lanes(k)], sigma.at[:, :, k, :], load_sem.at[which]))
            else:
                out.append(pltpu.make_async_copy(g_hbm.at[:, :, lanes(k)], tags.at[:, :, k, :], load_sem.at[which]))
        return out

    all_loads = [loads(w) for w in range(8)]
    for group in all_loads:
        for copy in group:
            copy.start()

    plan = [
        (has_cm, (c - 1, g), has_cp, e.at[pl.ds(1, 2), 0, pl.ds(0, sz)], xp),
        (has_hm, (c, g - 1), has_hp, e.at[pl.ds(0, 2), pl.ds(0, sx), 0], zp),
        (has_cp, (c + 1, g), has_cm, h.at[pl.ds(1, 2), sx, pl.ds(1, sz)], xm),
        (has_hp, (c, g + 1), has_hm, h.at[pl.ds(0, 2), pl.ds(1, sx), sz], zm),
        (has_cp & has_hm, (c + 1, g - 1), has_cm & has_hp, e.at[0, sx - 1, 0], cm),
        (has_cm & has_hp, (c - 1, g + 1), has_cp & has_hm, e.at[2, 0, sz - 1], cp),
    ]

    barrier = pltpu.get_barrier_semaphore()

    def greet(semaphore, device):
        pl.semaphore_signal(semaphore, inc=1, device_id=device, device_id_type=MESH)

    def along_col(semaphore):
        def one(i, _):
            greet(semaphore, (lax.rem(c + i, nc), g))
            return 0

        lax.fori_loop(1, nc, one, 0)

    def along_hgt(i, _):
        greet(barrier, (c, lax.rem(g + i, nh)))
        return 0

    lax.fori_loop(1, nh, along_hgt, 0)
    along_col(barrier)
    peers = nc + nh - 2
    for sends, device, _, _, _ in plan[4:]:
        @pl.when(sends)
        def _(device=device):
            greet(barrier, device)
        peers = peers + sends.astype(jnp.int32)
    zero_tile = jnp.zeros((8, 128), F32)
    for i in range(3):
        e[i, sx] = jnp.zeros((sz + 1, 8, 128), F32)
        h[i, 0] = jnp.zeros((sz + 1, 8, 128), F32)

    def clear(x, _):
        for i in range(3):
            e[i, x, sz] = zero_tile
            h[i, x + 1, 0] = zero_tile
        return 0

    lax.fori_loop(0, sx, clear, 0)
    pl.semaphore_wait(barrier, peers)
    along_col(ready)

    def copies(t):
        out = []
        for j, (sends, device, receives, src, buf) in enumerate(plan):
            out.append((sends, receives, pltpu.make_async_remote_copy(
                src_ref=src, dst_ref=buf.at[t], send_sem=ssem.at[t, j], recv_sem=rsem.at[t, j],
                device_id=device, device_id_type=MESH)))
        return out

    def update_h(x, nx, z0, nz):
        xs, xn, zs, zn, zw = pl.ds(x, nx), pl.ds(x + 1, nx), pl.ds(z0, nz), pl.ds(z0 + 1, nz), pl.ds(z0, nz + 1)
        ex, ey, ez = e[0, xs, zw], e[1, xs, zw], e[2, xs, zs]
        ey_x, ez_x = e[1, xn, zs], e[2, xn, zs]
        hx, hy, hz = h[0, xn, zn], h[1, xn, zn], h[2, xn, zn]
        ex, ex_z = ex[:, :nz], ex[:, 1:]
        ey, ey_z = ey[:, :nz], ey[:, 1:]
        hx = hx - COURANT * ((shifted_up(ez) - ez) - (ey_z - ey))
        hy = hy - COURANT * ((ex_z - ex) - (ez_x - ez))
        hz = hz - COURANT * ((ey_x - ey) - (shifted_up(ex) - ex))
        h[0, xn, zn] = hx
        h[1, xn, zn] = hy
        h[2, xn, zn] = hz

    def power_rows(x, z0, nz):
        return pl.ds(pl.multiple_of((x * sz + z0) * 8, 8), nz * 8)

    def update_e(x, nx, z0, nz):
        xs, xn, zs, zn, zw = pl.ds(x, nx), pl.ds(x + 1, nx), pl.ds(z0, nz), pl.ds(z0 + 1, nz), pl.ds(z0, nz + 1)
        hx, hy, hz = h[0, xn, zw], h[1, xn, zw], h[2, xn, zn]
        hy_x, hz_x = h[1, xs, zn], h[2, xs, zn]
        ex, ey, ez = e[0, xs, zs], e[1, xs, zs], e[2, xs, zs]
        a, b, s = ca[xs, zs], cb[xs, zs], sigma[xs, zs]
        lines = [power_rows(x + i, z0, nz) for i in range(nx)]
        p = [power[line].reshape(nz, 8, 128) for line in lines]
        hx_z, hx = hx[:, :nz], hx[:, 1:]
        hy_z, hy = hy[:, :nz], hy[:, 1:]
        ex = a * ex + b * ((hz - shifted_down(hz)) - (hy - hy_z))
        ey = a * ey + b * ((hx - hx_z) - (hz - hz_x))
        ez = a * ez + b * ((hy - hy_x) - (hx - shifted_down(hx)))
        e[0, xs, zs] = ex
        e[1, xs, zs] = ey
        e[2, xs, zs] = ez
        dissipated = s * (ex * ex + ey * ey + ez * ez)
        for i in range(nx):
            power[lines[i]] = (p[i] + dissipated[i]).reshape(nz * 8, 128)

    def over(x_lo, x_hi, nx, z_lo, z_hi, body):
        def at(i, _):
            body(x_lo + i * nx, nx, z_lo, z_hi - z_lo)
            return 0

        lax.fori_loop(0, (x_hi - x_lo) // nx, at, 0)

    def set_coefficients(x, nx, z0, nz):
        xs, zs = pl.ds(x, nx), pl.ds(z0, nz)
        s, a, b = coefficients(sigma[xs, zs], tags[xs, zs])
        sigma[xs, zs] = s
        ca[xs, zs] = a
        cb[xs, zs] = b
        for i in range(nx):
            power[power_rows(x + i, z0, nz)] = jnp.zeros((nz * 8, 128), F32)

    def corrections(t):
        @pl.when(has_cp)
        def _():
            h[1, sx, pl.ds(1, sz)] = h[1, sx, pl.ds(1, sz)] + COURANT * xp[t, 1]
            h[2, sx, pl.ds(1, sz)] = h[2, sx, pl.ds(1, sz)] - COURANT * xp[t, 0]

        @pl.when(has_cm)
        def _():
            h[1, 0, pl.ds(1, sz)] = xm[t, 0] + COURANT * e[2, 0, pl.ds(0, sz)]
            h[2, 0, pl.ds(1, sz)] = xm[t, 1] - COURANT * e[1, 0, pl.ds(0, sz)]

        @pl.when(has_cm & has_hp)
        def _():
            h[1, 0, sz] = h[1, 0, sz] - COURANT * cm[t]

        def rows(x, _):
            @pl.when(has_hp)
            def _():
                h[0, x + 1, sz] = h[0, x + 1, sz] + COURANT * zp[t, 1, x]
                h[1, x + 1, sz] = h[1, x + 1, sz] - COURANT * zp[t, 0, x]

            @pl.when(has_hm)
            def _():
                h[0, x + 1, 0] = zm[t, 0, x] + COURANT * e[1, x, 0]
                h[1, x + 1, 0] = zm[t, 1, x] - COURANT * e[0, x, 0]
            return 0

        lax.fori_loop(0, sx, rows, 0)

        @pl.when(has_cp & has_hm)
        def _():
            h[1, sx, 0] = h[1, sx, 0] + COURANT * cp[t]

    me = c * nh + g

    def partner(d):
        t = me ^ ((d * 11) % n_dev)
        return t, (t // nh, t % nh)

    def node_copy(d):
        t, device = partner(d)
        return pltpu.make_async_remote_copy(
            src_ref=nodes.at[t], dst_ref=recv_nodes.at[d], send_sem=node_out_sem, recv_sem=node_in_sem,
            device_id=device, device_id_type=MESH)

    def send_nodes(d, _):
        node_copy(d).start()
        return 0

    def block_copy(d):
        device = partner(d)[1]
        return pltpu.make_async_remote_copy(
            src_ref=send.at[d], dst_ref=recv.at[d], send_sem=out_sem,
            recv_sem=in_sem.at[d // GROUP], device_id=device, device_id_type=MESH)

    def gather(d):
        t = partner(d)[0]
        for r in range(cap):
            i = source[t, r]
            send[d, pl.ds(r, 1)] = power[pl.ds(i, 1)]

    for w in range(6):
        for copy in all_loads[w]:
            copy.wait()
    for t in range(STEPS):
        update_h(sx - 1, 1, 0, sz)
        update_h(0, sx - 1, sz - 1, 1)
        for sends, _, copy in copies(t):
            pl.when(sends)(copy.start)
        over(0, sx - 1, NXH, 0, sz - 1, update_h)
        if t == 0:
            for w in range(6, 8):
                for copy in all_loads[w]:
                    copy.wait()
            over(0, sx, 1, 0, sz, set_coefficients)
        over(1, sx - 1, NXE, 1, sz - 1, update_e)
        if t == 1:
            pl.semaphore_wait(ready, nc - 1)
            own_nodes = pltpu.make_async_copy(nodes.at[me], recv_nodes.at[0], local_sem.at[0])
            own_nodes.start()
            lax.fori_loop(1, n_dev, send_nodes, 0)
        for sends, receives, copy in copies(t):
            pl.when(sends)(copy.wait_send)
            pl.when(receives)(copy.wait_recv)
        corrections(t)
        update_e(0, 1, 0, sz)
        update_e(sx - 1, 1, 0, sz)
        update_e(1, sx - 2, 0, 1)
        update_e(1, sx - 2, sz - 1, 1)

    gather(0)
    gather(1)
    own = pltpu.make_async_copy(send.at[0], recv.at[0], local_sem.at[1])
    own.start()

    def exchange(d, _):
        gather(d)
        block_copy(d - 1).start()
        return 0

    lax.fori_loop(2, n_dev, exchange, 0)
    own.wait()
    own_nodes.wait()
    block_copy(n_dev - 1).start()
    others = pl.ds(0, n_dev - 1)
    pltpu.make_async_copy(recv_nodes.at[others], recv_nodes.at[others], node_in_sem).wait()
    pltpu.make_async_copy(recv_nodes.at[others], recv_nodes.at[others], node_out_sem).wait()

    n_nodes = enthalpy.shape[0]
    span = GROUP * cap
    count = lax.broadcasted_iota(jnp.int32, (n_nodes, span), 0).astype(F32) + 1.0

    def deposit(i, heat):
        tag = jnp.concatenate([recv_nodes[i * GROUP + j][:, :cap] for j in range(GROUP)], axis=1)
        pick = jnp.where(count == tag, 1.0, 0.0).astype(jnp.bfloat16)
        blocks = recv[pl.ds(i * GROUP, GROUP)].reshape(span, 128)
        high = blocks.astype(jnp.bfloat16)
        low = (blocks - high.astype(F32)).astype(jnp.bfloat16)
        both = jnp.dot(pick, jnp.concatenate([high, low], axis=1), preferred_element_type=F32)
        return heat + (both[:, :128] + both[:, 128:])

    def arrived(i, n):
        part = recv.at[pl.ds(0, n)]
        pltpu.make_async_copy(part, part, in_sem.at[i]).wait()

    def collect(i, heat):
        arrived(i, GROUP)
        return deposit(i, heat)

    arrived(0, GROUP - 1)
    heat = deposit(0, jnp.zeros((n_nodes, 128), F32))
    heat = lax.fori_loop(1, n_dev // GROUP, collect, heat)
    q = enthalpy[...] + (0.25 / STEPS) * heat
    out[...] = jnp.where(q < 0.0, q / 2.0, jnp.where(q > 1.0, (q - 1.0) / 3.0, 0.0))
    pltpu.make_async_copy(recv.at[others], recv.at[others], out_sem).wait()


def route_kernel(n_dev, cap, owner_ref, node_ref, source_ref, nodes_ref):
    rows = owner_ref.shape[0]
    who = lax.broadcasted_iota(jnp.int32, (n_dev, 128), 0)
    earlier = (lax.broadcasted_iota(jnp.int32, (128, 128), 0) < lax.broadcasted_iota(jnp.int32, (128, 128), 1)).astype(jnp.bfloat16)
    slot = lax.broadcasted_iota(jnp.int32, (128, 128), 0)
    lane = lax.broadcasted_iota(jnp.int32, (1, 128), 1).astype(F32)
    base = jnp.zeros((n_dev, 1), F32)
    sums = [jnp.zeros((n_dev, 128), F32) for _ in range(4)]
    for r in range(rows):
        own = owner_ref[pl.ds(r, 1), :]
        node = node_ref[pl.ds(r, 1), :] + 1
        hit = who == own
        hit_f = hit.astype(F32)
        hit_b = hit_f.astype(jnp.bfloat16)
        before = jnp.dot(hit_b, earlier, preferred_element_type=F32) + base
        rank = jnp.sum(hit_f * before, axis=0, keepdims=True).astype(jnp.int32)
        base = base + jnp.sum(hit_f, axis=1, keepdims=True)
        at = slot == rank
        values = (jnp.full((1, 128), float(r), F32), lane, (node // 16).astype(F32), (node % 16).astype(F32))
        for j, value in enumerate(values):
            sums[j] = sums[j] + lax.dot_general(
                hit_b, jnp.where(at, value, 0.0).astype(jnp.bfloat16), (((1,), (1,)), ((), ())), preferred_element_type=F32)
    source_ref[...] = (128.0 * sums[0] + sums[1]).astype(jnp.int32)
    nodes_ref[...] = (16.0 * sums[2] + sums[3]).reshape(nodes_ref.shape)


def store_kernel(e, h, e_hbm, h_hbm, sem):
    sx, sz = e_hbm.shape[1], e_hbm.shape[2]
    copies = []
    for i in range(3):
        for k in range(e_hbm.shape[3] // 128):
            copies.append(pltpu.make_async_copy(
                e.at[i, pl.ds(0, sx), pl.ds(0, sz), k, :], e_hbm.at[i, :, :, pl.ds(k * 128, 128)], sem))
            copies.append(pltpu.make_async_copy(
                h.at[i, pl.ds(1, sx), pl.ds(1, sz), k, :], h_hbm.at[i, :, :, pl.ds(k * 128, 128)], sem))
    for copy in copies:
        copy.start()
    for copy in copies:
        copy.wait()


def per_device(nc, nh, efield, hfield, cell_temp, region_tags, block_owner, block_node, node_enthalpy):
    sx, sz, sy = cell_temp.shape
    n_dev = nc * nh
    blocks = sx * sz * sy // 128
    cap = 2 * blocks // n_dev
    dma = pltpu.SemaphoreType.DMA

    def tiles(*shape):
        return pltpu.VMEM(shape + (8, 128), F32)

    def out(*shape):
        return jax.ShapeDtypeStruct(shape, F32)

    source, nodes = pl.pallas_call(
        lambda *refs: route_kernel(n_dev, cap, *refs),
        out_shape=(jax.ShapeDtypeStruct((n_dev, 128), jnp.int32), out(n_dev, 1, 128)),
        in_specs=[VMEM] * 2,
        out_specs=(VMEM, VMEM),
        name="route",
    )(block_owner.reshape(-1, 128), block_node.reshape(-1, 128))
    e, h, temp = pl.pallas_call(
        lambda *refs: fields_kernel(nc, nh, cap, *refs),
        out_shape=(tiles(3, sx + 1, sz + 1), tiles(3, sx + 1, sz + 1), out(*node_enthalpy.shape)),
        in_specs=[SMEM] + [HBM] * 4 + [VMEM, VMEM],
        out_specs=(VMEM, VMEM, VMEM),
        scratch_shapes=[
            pltpu.VMEM((sx * sz * 8, 128), F32), pltpu.VMEM((sx, sz, 8, 128), jnp.int32), tiles(sx, sz), tiles(sx, sz), tiles(sx, sz),
            tiles(STEPS, 2, sz), tiles(STEPS, 2, sx), tiles(STEPS, 2, sz), tiles(STEPS, 2, sx), tiles(STEPS), tiles(STEPS),
            pltpu.VMEM((n_dev, cap, 128), F32), pltpu.VMEM((n_dev, cap, 128), F32), pltpu.VMEM((n_dev, 1, 128), F32),
            dma((8,)), dma((STEPS, 6)), dma((STEPS, 6)), pltpu.SemaphoreType.REGULAR, dma((2,)), dma, dma((n_dev // GROUP,)), dma, dma,
        ],
        compiler_params=pltpu.CompilerParams(collective_id=0, has_side_effects=True, vmem_limit_bytes=48 << 20),
        name="fields",
    )(source, efield, hfield, cell_temp, region_tags, nodes, node_enthalpy)
    e_out, h_out = pl.pallas_call(
        store_kernel,
        out_shape=(out(3, sx, sz, sy), out(3, sx, sz, sy)),
        in_specs=[VMEM, VMEM],
        out_specs=(HBM, HBM),
        scratch_shapes=[dma],
        compiler_params=pltpu.CompilerParams(vmem_limit_bytes=24 << 20),
        name="store",
    )(e, h)
    return e_out, h_out, temp


def solution(mesh):
    placed = (
        P(None, "col", "hgt", None),
        P(None, "col", "hgt", None),
        P("col", "hgt", None),
        P("col", "hgt", None),
        P("col", "hgt", None, None, None, None),
        P("col", "hgt", None, None, None),
        P(("col", "hgt"), None),
    )
    nc, nh = mesh.shape["col"], mesh.shape["hgt"]
    return jax.shard_map(
        lambda *args: per_device(nc, nh, *args),
        mesh=mesh,
        in_specs=placed,
        out_specs=(P(None, "col", "hgt", None), P(None, "col", "hgt", None), P(("col", "hgt"), None)),
        check_vma=False,
    )
```

```python
import jax
import jax.numpy as jnp
from jax import lax
from jax.experimental import pallas as pl
from jax.experimental.pallas import tpu as pltpu
from jax.sharding import PartitionSpec as P

STEPS = 4
COURANT = 0.55
NXH = 1
NXE = 1
GROUP = 8
MESH = pl.DeviceIdType.MESH
F32 = jnp.float32
HBM = pl.BlockSpec(memory_space=pltpu.HBM)
VMEM = pl.BlockSpec(memory_space=pltpu.VMEM)


def shifted_up(f):
    axis = f.ndim - 1
    lane = lax.broadcasted_iota(jnp.int32, f.shape, axis)
    sub = lax.broadcasted_iota(jnp.int32, f.shape, axis - 1)
    r = pltpu.roll(f, 127, axis)
    u = pltpu.roll(r, 7, axis - 1)
    return jnp.where(lane < 127, r, jnp.where(sub < 7, u, 0.0))


def shifted_down(f):
    axis = f.ndim - 1
    lane = lax.broadcasted_iota(jnp.int32, f.shape, axis)
    sub = lax.broadcasted_iota(jnp.int32, f.shape, axis - 1)
    r = pltpu.roll(f, 1, axis)
    u = pltpu.roll(r, 1, axis - 1)
    return jnp.where(lane > 0, r, jnp.where(sub > 0, u, 0.0))


def coefficients(temp, tags):
    frac = 1.0 / (1.0 + jnp.exp(-2.0 * temp))
    lean = tags == 0
    fat = tags == 1
    eps_frozen = jnp.where(lean, 4.0, jnp.where(fat, 2.5, 5.0))
    eps_span = jnp.where(lean, 46.0, jnp.where(fat, 3.5, 5.0))
    sig_frozen = jnp.where(lean, 0.2, jnp.where(fat, 0.05, 0.1))
    sig_span = jnp.where(lean, 7.8, jnp.where(fat, 0.35, 0.9))
    eps2 = 2.0 * (eps_frozen + eps_span * frac)
    sigma = sig_frozen + sig_span * frac
    half = sigma * COURANT
    inv = 1.0 / (eps2 + half)
    return sigma, (eps2 - half) * inv, (2.0 * COURANT) * inv


def route(n_dev, cap, owner_ref, node_ref, source_ref, nodes_ref):
    sx, nk, sz = owner_ref.shape
    per = max(p for p in range(1, 128 // sz + 1) if sx % p == 0)
    who = lax.broadcasted_iota(jnp.int32, (n_dev, 128), 0)
    earlier = (lax.broadcasted_iota(jnp.int32, (128, 128), 0) < lax.broadcasted_iota(jnp.int32, (128, 128), 1)).astype(jnp.bfloat16)
    slot = lax.broadcasted_iota(jnp.int32, (cap, 128), 0)
    lane = lax.broadcasted_iota(jnp.int32, (1, 128), 1).astype(F32)
    first = lax.broadcasted_iota(jnp.int32, (1, 4 * cap), 1) < cap
    base = jnp.zeros((n_dev, 1), F32)
    sums = jnp.zeros((n_dev, 4 * cap), F32)
    for q in range(sx // per):
        fill = jnp.full((nk, 128 - per * sz), -1, jnp.int32)
        owners = jnp.concatenate([owner_ref[q * per + i] for i in range(per)] + [fill], axis=1)
        tags = jnp.concatenate([node_ref[q * per + i] for i in range(per)] + [fill], axis=1) + 1
        tags_hi = (tags // 16).astype(F32)
        tags_lo = (tags % 16).astype(F32)
        for k in range(nk):
            hit = who == owners[k : k + 1]
            hit_f = hit.astype(F32)
            hit_b = hit_f.astype(jnp.bfloat16)
            before = jnp.dot(hit_b, earlier, preferred_element_type=F32) + base
            rank = jnp.sum(hit_f * before, axis=0, keepdims=True).astype(jnp.int32)
            base = base + jnp.sum(hit_f, axis=1, keepdims=True)
            at = slot == rank
            values = (1.0, lane, tags_hi[k : k + 1], tags_lo[k : k + 1])
            table = jnp.concatenate([jnp.where(at, value, 0.0) for value in values], axis=0).astype(jnp.bfloat16)
            got = lax.dot_general(hit_b, table, (((1,), (1,)), ((), ())), preferred_element_type=F32)
            sums = sums + got * jnp.where(first, float(q * per * sz * nk + k), 1.0)
    source_ref[:, :cap] = (sums[:, :cap] + float(nk) * sums[:, cap : 2 * cap]).astype(jnp.int32)
    tag = 16.0 * sums[:, 2 * cap : 3 * cap] + sums[:, 3 * cap :]
    nodes_ref[...] = jnp.concatenate([tag, jnp.zeros((n_dev, 128 - cap), F32)], axis=1).reshape(n_dev, 1, 128)


def fields_kernel(nc, nh, cap, e_hbm, h_hbm, t_hbm, g_hbm, owner, node, e, h, heat_out,
                  source_vmem, source, nodes, power, tags, sigma, ca, cb, xp, zp, xm, zm, cm, cp, send, recv, recv_nodes,
                  load_sem, ssem, rsem, ready, local_sem, out_sem, in_sem, node_out_sem, node_in_sem):
    n_dev = nc * nh
    sx, sz = t_hbm.shape[0], t_hbm.shape[1]
    nk = t_hbm.shape[2] // 128
    c = lax.axis_index("col")
    g = lax.axis_index("hgt")
    has_cp, has_cm = c < nc - 1, c > 0
    has_hp, has_hm = g < nh - 1, g > 0

    def lanes(k):
        return pl.ds(k * 128, 128)

    def loads(which):
        out = []
        for k in range(nk):
            if which < 3:
                out.append(pltpu.make_async_copy(
                    e_hbm.at[which, :, :, lanes(k)], e.at[which, pl.ds(0, sx), pl.ds(0, sz), k, :], load_sem.at[which]))
            elif which < 6:
                out.append(pltpu.make_async_copy(
                    h_hbm.at[which - 3, :, :, lanes(k)], h.at[which - 3, pl.ds(1, sx), pl.ds(1, sz), k, :], load_sem.at[which]))
            elif which == 6:
                out.append(pltpu.make_async_copy(t_hbm.at[:, :, lanes(k)], sigma.at[:, :, k, :], load_sem.at[which]))
            else:
                out.append(pltpu.make_async_copy(g_hbm.at[:, :, lanes(k)], tags.at[:, :, k, :], load_sem.at[which]))
        return out

    all_loads = [loads(w) for w in range(8)]
    for w in (6, 7, 0, 1, 2, 3, 4, 5):
        for copy in all_loads[w]:
            copy.start()

    plan = [
        (has_cm, (c - 1, g), has_cp, e.at[pl.ds(1, 2), 0, pl.ds(0, sz)], xp),
        (has_hm, (c, g - 1), has_hp, e.at[pl.ds(0, 2), pl.ds(0, sx), 0], zp),
        (has_cp, (c + 1, g), has_cm, h.at[pl.ds(1, 2), sx, pl.ds(1, sz)], xm),
        (has_hp, (c, g + 1), has_hm, h.at[pl.ds(0, 2), pl.ds(1, sx), sz], zm),
        (has_cp & has_hm, (c + 1, g - 1), has_cm & has_hp, e.at[0, sx - 1, 0], cm),
        (has_cm & has_hp, (c - 1, g + 1), has_cp & has_hm, e.at[2, 0, sz - 1], cp),
    ]

    barrier = pltpu.get_barrier_semaphore()

    def greet(semaphore, device):
        pl.semaphore_signal(semaphore, inc=1, device_id=device, device_id_type=MESH)

    def along_col(semaphore):
        def one(i, _):
            greet(semaphore, (lax.rem(c + i, nc), g))
            return 0

        lax.fori_loop(1, nc, one, 0)

    def along_hgt(i, _):
        greet(barrier, (c, lax.rem(g + i, nh)))
        return 0

    lax.fori_loop(1, nh, along_hgt, 0)
    along_col(barrier)
    peers = nc + nh - 2
    for sends, device, _, _, _ in plan[4:]:
        @pl.when(sends)
        def _(device=device):
            greet(barrier, device)
        peers = peers + sends.astype(jnp.int32)
    zero_tile = jnp.zeros((8, 128), F32)
    for i in range(3):
        e[i, sx] = jnp.zeros((sz + 1, 8, 128), F32)
        h[i, 0] = jnp.zeros((sz + 1, 8, 128), F32)

    def clear(x, _):
        for i in range(3):
            e[i, x, sz] = zero_tile
            h[i, x + 1, 0] = zero_tile
        return 0

    lax.fori_loop(0, sx, clear, 0)
    def copies(t):
        out = []
        for j, (sends, device, receives, src, buf) in enumerate(plan):
            out.append((sends, receives, pltpu.make_async_remote_copy(
                src_ref=src, dst_ref=buf.at[t], send_sem=ssem.at[t, j], recv_sem=rsem.at[t, j],
                device_id=device, device_id_type=MESH)))
        return out

    def update_h(x, nx, z0, nz):
        xs, xn, zs, zn, zw = pl.ds(x, nx), pl.ds(x + 1, nx), pl.ds(z0, nz), pl.ds(z0 + 1, nz), pl.ds(z0, nz + 1)
        ex, ey, ez = e[0, xs, zw], e[1, xs, zw], e[2, xs, zs]
        ey_x, ez_x = e[1, xn, zs], e[2, xn, zs]
        hx, hy, hz = h[0, xn, zn], h[1, xn, zn], h[2, xn, zn]
        ex, ex_z = ex[:, :nz], ex[:, 1:]
        ey, ey_z = ey[:, :nz], ey[:, 1:]
        hx = hx - COURANT * ((shifted_up(ez) - ez) - (ey_z - ey))
        hy = hy - COURANT * ((ex_z - ex) - (ez_x - ez))
        hz = hz - COURANT * ((ey_x - ey) - (shifted_up(ex) - ex))
        h[0, xn, zn] = hx
        h[1, xn, zn] = hy
        h[2, xn, zn] = hz

    def power_rows(x, z0, nz):
        return pl.ds(pl.multiple_of((x * sz + z0) * 8, 8), nz * 8)

    def update_e(x, nx, z0, nz):
        xs, xn, zs, zn, zw = pl.ds(x, nx), pl.ds(x + 1, nx), pl.ds(z0, nz), pl.ds(z0 + 1, nz), pl.ds(z0, nz + 1)
        hx, hy, hz = h[0, xn, zw], h[1, xn, zw], h[2, xn, zn]
        hy_x, hz_x = h[1, xs, zn], h[2, xs, zn]
        ex, ey, ez = e[0, xs, zs], e[1, xs, zs], e[2, xs, zs]
        a, b, s = ca[xs, zs], cb[xs, zs], sigma[xs, zs]
        lines = [power_rows(x + i, z0, nz) for i in range(nx)]
        p = [power[line].reshape(nz, 8, 128) for line in lines]
        hx_z, hx = hx[:, :nz], hx[:, 1:]
        hy_z, hy = hy[:, :nz], hy[:, 1:]
        ex = a * ex + b * ((hz - shifted_down(hz)) - (hy - hy_z))
        ey = a * ey + b * ((hx - hx_z) - (hz - hz_x))
        ez = a * ez + b * ((hy - hy_x) - (hx - shifted_down(hx)))
        e[0, xs, zs] = ex
        e[1, xs, zs] = ey
        e[2, xs, zs] = ez
        dissipated = s * (ex * ex + ey * ey + ez * ez)
        for i in range(nx):
            power[lines[i]] = (p[i] + dissipated[i]).reshape(nz * 8, 128)

    def over(x_lo, x_hi, nx, z_lo, z_hi, body):
        def at(i, _):
            body(x_lo + i * nx, nx, z_lo, z_hi - z_lo)
            return 0

        lax.fori_loop(0, (x_hi - x_lo) // nx, at, 0)

    def set_coefficients(x, nx, z0, nz):
        xs, zs = pl.ds(x, nx), pl.ds(z0, nz)
        s, a, b = coefficients(sigma[xs, zs], tags[xs, zs])
        sigma[xs, zs] = s
        ca[xs, zs] = a
        cb[xs, zs] = b
        for i in range(nx):
            power[power_rows(x + i, z0, nz)] = jnp.zeros((nz * 8, 128), F32)

    def corrections(t):
        @pl.when(has_cp)
        def _():
            h[1, sx, pl.ds(1, sz)] = h[1, sx, pl.ds(1, sz)] + COURANT * xp[t, 1]
            h[2, sx, pl.ds(1, sz)] = h[2, sx, pl.ds(1, sz)] - COURANT * xp[t, 0]

        @pl.when(has_cm)
        def _():
            h[1, 0, pl.ds(1, sz)] = xm[t, 0] + COURANT * e[2, 0, pl.ds(0, sz)]
            h[2, 0, pl.ds(1, sz)] = xm[t, 1] - COURANT * e[1, 0, pl.ds(0, sz)]

        @pl.when(has_cm & has_hp)
        def _():
            h[1, 0, sz] = h[1, 0, sz] - COURANT * cm[t]

        def rows(x, _):
            @pl.when(has_hp)
            def _():
                h[0, x + 1, sz] = h[0, x + 1, sz] + COURANT * zp[t, 1, x]
                h[1, x + 1, sz] = h[1, x + 1, sz] - COURANT * zp[t, 0, x]

            @pl.when(has_hm)
            def _():
                h[0, x + 1, 0] = zm[t, 0, x] + COURANT * e[1, x, 0]
                h[1, x + 1, 0] = zm[t, 1, x] - COURANT * e[0, x, 0]
            return 0

        lax.fori_loop(0, sx, rows, 0)

        @pl.when(has_cp & has_hm)
        def _():
            h[1, sx, 0] = h[1, sx, 0] + COURANT * cp[t]

    me = c * nh + g

    def partner(d):
        t = me ^ ((d * 11) % n_dev)
        return t, (t // nh, t % nh)

    def node_copy(d):
        t, device = partner(d)
        return pltpu.make_async_remote_copy(
            src_ref=nodes.at[t], dst_ref=recv_nodes.at[d], send_sem=node_out_sem, recv_sem=node_in_sem,
            device_id=device, device_id_type=MESH)

    def send_nodes(d, _):
        node_copy(d).start()
        return 0

    def block_copy(d):
        device = partner(d)[1]
        return pltpu.make_async_remote_copy(
            src_ref=send.at[d], dst_ref=recv.at[d], send_sem=out_sem,
            recv_sem=in_sem.at[d // GROUP], device_id=device, device_id_type=MESH)

    def gather(d):
        t = partner(d)[0]
        for r in range(cap):
            i = jnp.clip(source[t, r], 0, sx * sz * 8 - 1)
            send[d, pl.ds(r, 1)] = power[pl.ds(i, 1)]

    route(n_dev, cap, owner, node, source_vmem, nodes)
    for w in range(6, 8):
        for copy in all_loads[w]:
            copy.wait()
    over(0, sx, 1, 0, sz, set_coefficients)
    to_smem = pltpu.make_async_copy(source_vmem, source, local_sem.at[2])
    to_smem.start()
    to_smem.wait()
    pl.semaphore_wait(barrier, peers)
    along_col(ready)
    for w in range(6):
        for copy in all_loads[w]:
            copy.wait()
    for t in range(STEPS):
        update_h(sx - 1, 1, 0, sz)
        update_h(0, sx - 1, sz - 1, 1)
        for sends, _, copy in copies(t):
            pl.when(sends)(copy.start)
        over(0, sx - 1, NXH, 0, sz - 1, update_h)
        over(1, sx - 1, NXE, 1, sz - 1, update_e)
        if t == 1:
            pl.semaphore_wait(ready, nc - 1)
            own_nodes = pltpu.make_async_copy(nodes.at[me], recv_nodes.at[0], local_sem.at[0])
            own_nodes.start()
            lax.fori_loop(1, n_dev, send_nodes, 0)
        for sends, receives, copy in copies(t):
            pl.when(sends)(copy.wait_send)
            pl.when(receives)(copy.wait_recv)
        corrections(t)
        update_e(0, 1, 0, sz)
        update_e(sx - 1, 1, 0, sz)
        update_e(1, sx - 2, 0, 1)
        update_e(1, sx - 2, sz - 1, 1)

    gather(0)
    gather(1)
    own = pltpu.make_async_copy(send.at[0], recv.at[0], local_sem.at[1])
    own.start()

    def exchange(d, _):
        gather(d)
        block_copy(d - 1).start()
        return 0

    lax.fori_loop(2, n_dev, exchange, 0)
    own.wait()
    own_nodes.wait()
    block_copy(n_dev - 1).start()
    others = pl.ds(0, n_dev - 1)
    pltpu.make_async_copy(recv_nodes.at[others], recv_nodes.at[others], node_in_sem).wait()
    pltpu.make_async_copy(recv_nodes.at[others], recv_nodes.at[others], node_out_sem).wait()

    n_nodes = heat_out.shape[0]
    span = GROUP * cap
    count = lax.broadcasted_iota(jnp.int32, (n_nodes, span), 0).astype(F32) + 1.0

    def deposit(i, heat):
        tag = jnp.concatenate([recv_nodes[i * GROUP + j][:, :cap] for j in range(GROUP)], axis=1)
        pick = jnp.where(count == tag, 1.0, 0.0).astype(jnp.bfloat16)
        blocks = recv[pl.ds(i * GROUP, GROUP)].reshape(span, 128)
        high = blocks.astype(jnp.bfloat16)
        low = (blocks - high.astype(F32)).astype(jnp.bfloat16)
        both = jnp.dot(pick, jnp.concatenate([high, low], axis=1), preferred_element_type=F32)
        return heat + (both[:, :128] + both[:, 128:])

    def arrived(i, n):
        part = recv.at[pl.ds(0, n)]
        pltpu.make_async_copy(part, part, in_sem.at[i]).wait()

    def collect(i, heat):
        arrived(i, GROUP)
        return deposit(i, heat)

    arrived(0, GROUP - 1)
    heat = deposit(0, jnp.zeros((n_nodes, 128), F32))
    heat = lax.fori_loop(1, n_dev // GROUP, collect, heat)
    heat_out[...] = heat
    pltpu.make_async_copy(recv.at[others], recv.at[others], out_sem).wait()


def store_kernel(e, h, heat, enthalpy, e_hbm, h_hbm, temp, sem):
    sx, sz = e_hbm.shape[1], e_hbm.shape[2]
    copies = []
    for i in range(3):
        for k in range(e_hbm.shape[3] // 128):
            copies.append(pltpu.make_async_copy(
                e.at[i, pl.ds(0, sx), pl.ds(0, sz), k, :], e_hbm.at[i, :, :, pl.ds(k * 128, 128)], sem))
            copies.append(pltpu.make_async_copy(
                h.at[i, pl.ds(1, sx), pl.ds(1, sz), k, :], h_hbm.at[i, :, :, pl.ds(k * 128, 128)], sem))
    for copy in copies:
        copy.start()
    q = enthalpy[...] + (0.25 / STEPS) * heat[...]
    temp[...] = jnp.where(q < 0.0, q / 2.0, jnp.where(q > 1.0, (q - 1.0) / 3.0, 0.0))
    for copy in copies:
        copy.wait()


def per_device(nc, nh, efield, hfield, cell_temp, region_tags, block_owner, block_node, node_enthalpy):
    sx, sz, sy = cell_temp.shape
    n_dev = nc * nh
    blocks = sx * sz * sy // 128
    cap = 2 * blocks // n_dev
    dma = pltpu.SemaphoreType.DMA

    def tiles(*shape):
        return pltpu.VMEM(shape + (8, 128), F32)

    def out(*shape):
        return jax.ShapeDtypeStruct(shape, F32)

    def native(table):
        return table.reshape(sx, sz, sy // 128).transpose(0, 2, 1)

    e, h, heat = pl.pallas_call(
        lambda *refs: fields_kernel(nc, nh, cap, *refs),
        out_shape=(tiles(3, sx + 1, sz + 1), tiles(3, sx + 1, sz + 1), pltpu.VMEM(node_enthalpy.shape, F32)),
        in_specs=[HBM] * 4 + [VMEM, VMEM],
        out_specs=(VMEM, VMEM, VMEM),
        scratch_shapes=[
            pltpu.VMEM((n_dev, 128), jnp.int32), pltpu.SMEM((n_dev, 128), jnp.int32), pltpu.VMEM((n_dev, 1, 128), F32),
            pltpu.VMEM((sx * sz * 8, 128), F32), pltpu.VMEM((sx, sz, 8, 128), jnp.int32), tiles(sx, sz), tiles(sx, sz), tiles(sx, sz),
            tiles(STEPS, 2, sz), tiles(STEPS, 2, sx), tiles(STEPS, 2, sz), tiles(STEPS, 2, sx), tiles(STEPS), tiles(STEPS),
            pltpu.VMEM((n_dev, cap, 128), F32), pltpu.VMEM((n_dev, cap, 128), F32), pltpu.VMEM((n_dev, 1, 128), F32),
            dma((8,)), dma((STEPS, 6)), dma((STEPS, 6)), pltpu.SemaphoreType.REGULAR, dma((3,)), dma, dma((n_dev // GROUP,)), dma, dma,
        ],
        compiler_params=pltpu.CompilerParams(collective_id=0, has_side_effects=True, vmem_limit_bytes=48 << 20),
        name="fields",
    )(efield, hfield, cell_temp, region_tags, native(block_owner), native(block_node))
    return pl.pallas_call(
        store_kernel,
        out_shape=(out(3, sx, sz, sy), out(3, sx, sz, sy), out(*node_enthalpy.shape)),
        in_specs=[VMEM] * 4,
        out_specs=(HBM, HBM, VMEM),
        scratch_shapes=[dma],
        compiler_params=pltpu.CompilerParams(vmem_limit_bytes=24 << 20),
        name="store",
    )(e, h, heat, node_enthalpy)


def solution(mesh):
    placed = (
        P(None, "col", "hgt", None),
        P(None, "col", "hgt", None),
        P("col", "hgt", None),
        P("col", "hgt", None),
        P("col", "hgt", None, None, None, None),
        P("col", "hgt", None, None, None),
        P(("col", "hgt"), None),
    )
    nc, nh = mesh.shape["col"], mesh.shape["hgt"]
    return jax.shard_map(
        lambda *args: per_device(nc, nh, *args),
        mesh=mesh,
        in_specs=placed,
        out_specs=(P(None, "col", "hgt", None), P(None, "col", "hgt", None), P(("col", "hgt"), None)),
        check_vma=False,
    )
```

```python
import jax
import jax.numpy as jnp
from jax import lax
from jax.experimental import pallas as pl
from jax.experimental.pallas import tpu as pltpu
from jax.sharding import PartitionSpec as P

STEPS = 4
COURANT = 0.55
GROUP = 8
MESH = pl.DeviceIdType.MESH
F32 = jnp.float32
HBM = pl.BlockSpec(memory_space=pltpu.HBM)
VMEM = pl.BlockSpec(memory_space=pltpu.VMEM)


def shifted_up(f):
    axis = f.ndim - 1
    lane = lax.broadcasted_iota(jnp.int32, f.shape, axis)
    sub = lax.broadcasted_iota(jnp.int32, f.shape, axis - 1)
    r = pltpu.roll(f, 127, axis)
    u = pltpu.roll(r, 7, axis - 1)
    return jnp.where(lane < 127, r, jnp.where(sub < 7, u, 0.0))


def shifted_down(f):
    axis = f.ndim - 1
    lane = lax.broadcasted_iota(jnp.int32, f.shape, axis)
    sub = lax.broadcasted_iota(jnp.int32, f.shape, axis - 1)
    r = pltpu.roll(f, 1, axis)
    u = pltpu.roll(r, 1, axis - 1)
    return jnp.where(lane > 0, r, jnp.where(sub > 0, u, 0.0))


def coefficients(temp, tags):
    frac = 1.0 / (1.0 + jnp.exp(-2.0 * temp))
    lean = tags == 0
    fat = tags == 1
    eps_frozen = jnp.where(lean, 4.0, jnp.where(fat, 2.5, 5.0))
    eps_span = jnp.where(lean, 46.0, jnp.where(fat, 3.5, 5.0))
    sig_frozen = jnp.where(lean, 0.2, jnp.where(fat, 0.05, 0.1))
    sig_span = jnp.where(lean, 7.8, jnp.where(fat, 0.35, 0.9))
    eps2 = 2.0 * (eps_frozen + eps_span * frac)
    sigma = sig_frozen + sig_span * frac
    half = sigma * COURANT
    inv = 1.0 / (eps2 + half)
    return sigma, (eps2 - half) * inv, (2.0 * COURANT) * inv


def route(n_dev, cap, owner_ref, node_ref, source_ref, nodes_ref):
    sx, nk, sz = owner_ref.shape
    per = max(p for p in range(1, 128 // sz + 1) if sx % p == 0)
    who = lax.broadcasted_iota(jnp.int32, (n_dev, 128), 0)
    earlier = (lax.broadcasted_iota(jnp.int32, (128, 128), 0) < lax.broadcasted_iota(jnp.int32, (128, 128), 1)).astype(jnp.bfloat16)
    slot = lax.broadcasted_iota(jnp.int32, (cap, 128), 0)
    lane = lax.broadcasted_iota(jnp.int32, (1, 128), 1).astype(F32)
    first = lax.broadcasted_iota(jnp.int32, (1, 4 * cap), 1) < cap
    base = jnp.zeros((n_dev, 1), F32)
    sums = jnp.zeros((n_dev, 4 * cap), F32)
    for q in range(sx // per):
        fill = jnp.full((nk, 128 - per * sz), -1, jnp.int32)
        owners = jnp.concatenate([owner_ref[q * per + i] for i in range(per)] + [fill], axis=1)
        tags = jnp.concatenate([node_ref[q * per + i] for i in range(per)] + [fill], axis=1) + 1
        tags_hi = (tags // 16).astype(F32)
        tags_lo = (tags % 16).astype(F32)
        for k in range(nk):
            hit = who == owners[k : k + 1]
            hit_f = hit.astype(F32)
            hit_b = hit_f.astype(jnp.bfloat16)
            before = jnp.dot(hit_b, earlier, preferred_element_type=F32) + base
            rank = jnp.sum(hit_f * before, axis=0, keepdims=True).astype(jnp.int32)
            base = base + jnp.sum(hit_f, axis=1, keepdims=True)
            at = slot == rank
            values = (1.0, lane, tags_hi[k : k + 1], tags_lo[k : k + 1])
            table = jnp.concatenate([jnp.where(at, value, 0.0) for value in values], axis=0).astype(jnp.bfloat16)
            got = lax.dot_general(hit_b, table, (((1,), (1,)), ((), ())), preferred_element_type=F32)
            sums = sums + got * jnp.where(first, float(q * per * sz * nk + k), 1.0)
    source_ref[:, :cap] = (sums[:, :cap] + float(nk) * sums[:, cap : 2 * cap]).astype(jnp.int32)
    tag = 16.0 * sums[:, 2 * cap : 3 * cap] + sums[:, 3 * cap :]
    nodes_ref[...] = jnp.concatenate([tag, jnp.zeros((n_dev, 128 - cap), F32)], axis=1).reshape(n_dev, 1, 128)


def fields_kernel(nc, nh, cap, e_hbm, h_hbm, t_hbm, g_hbm, owner, node, e, h, heat_out,
                  source_vmem, source, nodes, power, tags, sigma, ca, cb, xp, zp, xm, zm, cm, cp, send, recv, recv_nodes,
                  load_sem, ssem, rsem, ready, local_sem, out_sem, in_sem, node_out_sem, node_in_sem):
    n_dev = nc * nh
    sx, sz = t_hbm.shape[0], t_hbm.shape[1]
    nk = t_hbm.shape[2] // 128
    c = lax.axis_index("col")
    g = lax.axis_index("hgt")
    planes_h = max(p for p in (1, 2, 3) if (sx - 1) % p == 0)
    has_cp, has_cm = c < nc - 1, c > 0
    has_hp, has_hm = g < nh - 1, g > 0

    def lanes(k):
        return pl.ds(k * 128, 128)

    def loads(which):
        out = []
        for k in range(nk):
            if which < 3:
                out.append(pltpu.make_async_copy(
                    e_hbm.at[which, :, :, lanes(k)], e.at[which, pl.ds(0, sx), pl.ds(0, sz), k, :], load_sem.at[which]))
            elif which < 6:
                out.append(pltpu.make_async_copy(
                    h_hbm.at[which - 3, :, :, lanes(k)], h.at[which - 3, pl.ds(1, sx), pl.ds(1, sz), k, :], load_sem.at[which]))
            elif which == 6:
                out.append(pltpu.make_async_copy(t_hbm.at[:, :, lanes(k)], sigma.at[:, :, k, :], load_sem.at[which]))
            else:
                out.append(pltpu.make_async_copy(g_hbm.at[:, :, lanes(k)], tags.at[:, :, k, :], load_sem.at[which]))
        return out

    all_loads = [loads(w) for w in range(8)]
    for w in (6, 7, 0, 1, 2, 3, 4, 5):
        for copy in all_loads[w]:
            copy.start()

    plan = [
        (has_cm, (c - 1, g), has_cp, e.at[pl.ds(1, 2), 0, pl.ds(0, sz)], xp),
        (has_hm, (c, g - 1), has_hp, e.at[pl.ds(0, 2), pl.ds(0, sx), 0], zp),
        (has_cp, (c + 1, g), has_cm, h.at[pl.ds(1, 2), sx, pl.ds(1, sz)], xm),
        (has_hp, (c, g + 1), has_hm, h.at[pl.ds(0, 2), pl.ds(1, sx), sz], zm),
        (has_cp & has_hm, (c + 1, g - 1), has_cm & has_hp, e.at[0, sx - 1, 0], cm),
        (has_cm & has_hp, (c - 1, g + 1), has_cp & has_hm, e.at[2, 0, sz - 1], cp),
    ]

    barrier = pltpu.get_barrier_semaphore()

    def greet(semaphore, device):
        pl.semaphore_signal(semaphore, inc=1, device_id=device, device_id_type=MESH)

    def along_col(semaphore):
        def one(i, _):
            greet(semaphore, (lax.rem(c + i, nc), g))
            return 0

        lax.fori_loop(1, nc, one, 0)

    def along_hgt(i, _):
        greet(barrier, (c, lax.rem(g + i, nh)))
        return 0

    lax.fori_loop(1, nh, along_hgt, 0)
    along_col(barrier)
    peers = nc + nh - 2
    for sends, device, _, _, _ in plan[4:]:
        @pl.when(sends)
        def _(device=device):
            greet(barrier, device)
        peers = peers + sends.astype(jnp.int32)
    zero_tile = jnp.zeros((8, 128), F32)
    for i in range(3):
        e[i, sx] = jnp.zeros((sz + 1, 8, 128), F32)
        h[i, 0] = jnp.zeros((sz + 1, 8, 128), F32)

    def clear(x, _):
        for i in range(3):
            e[i, x, sz] = zero_tile
            h[i, x + 1, 0] = zero_tile
        return 0

    lax.fori_loop(0, sx, clear, 0)
    def copies(t):
        out = []
        for j, (sends, device, receives, src, buf) in enumerate(plan):
            out.append((sends, receives, pltpu.make_async_remote_copy(
                src_ref=src, dst_ref=buf.at[t], send_sem=ssem.at[t, j], recv_sem=rsem.at[t, j],
                device_id=device, device_id_type=MESH)))
        return out

    def update_h(x, nx, z0, nz):
        xs, xn, zs, zn, zw = pl.ds(x, nx), pl.ds(x + 1, nx), pl.ds(z0, nz), pl.ds(z0 + 1, nz), pl.ds(z0, nz + 1)
        ex, ey, ez = e[0, xs, zw], e[1, xs, zw], e[2, xs, zs]
        ey_x, ez_x = e[1, xn, zs], e[2, xn, zs]
        hx, hy, hz = h[0, xn, zn], h[1, xn, zn], h[2, xn, zn]
        ex, ex_z = ex[:, :nz], ex[:, 1:]
        ey, ey_z = ey[:, :nz], ey[:, 1:]
        hx = hx - COURANT * ((shifted_up(ez) - ez) - (ey_z - ey))
        hy = hy - COURANT * ((ex_z - ex) - (ez_x - ez))
        hz = hz - COURANT * ((ey_x - ey) - (shifted_up(ex) - ex))
        h[0, xn, zn] = hx
        h[1, xn, zn] = hy
        h[2, xn, zn] = hz

    def power_rows(x, z0, nz):
        return pl.ds(pl.multiple_of((x * sz + z0) * 8, 8), nz * 8)

    def update_e(x, nx, z0, nz):
        xs, xn, zs, zn, zw = pl.ds(x, nx), pl.ds(x + 1, nx), pl.ds(z0, nz), pl.ds(z0 + 1, nz), pl.ds(z0, nz + 1)
        hx, hy, hz = h[0, xn, zw], h[1, xn, zw], h[2, xn, zn]
        hy_x, hz_x = h[1, xs, zn], h[2, xs, zn]
        ex, ey, ez = e[0, xs, zs], e[1, xs, zs], e[2, xs, zs]
        a, b, s = ca[xs, zs], cb[xs, zs], sigma[xs, zs]
        lines = [power_rows(x + i, z0, nz) for i in range(nx)]
        p = [power[line].reshape(nz, 8, 128) for line in lines]
        hx_z, hx = hx[:, :nz], hx[:, 1:]
        hy_z, hy = hy[:, :nz], hy[:, 1:]
        ex = a * ex + b * ((hz - shifted_down(hz)) - (hy - hy_z))
        ey = a * ey + b * ((hx - hx_z) - (hz - hz_x))
        ez = a * ez + b * ((hy - hy_x) - (hx - shifted_down(hx)))
        e[0, xs, zs] = ex
        e[1, xs, zs] = ey
        e[2, xs, zs] = ez
        dissipated = s * (ex * ex + ey * ey + ez * ez)
        for i in range(nx):
            power[lines[i]] = (p[i] + dissipated[i]).reshape(nz * 8, 128)

    def update_e_in_halves(x, nx, z0, nz):
        update_e(x, nx, z0, nz // 2)
        update_e(x, nx, z0 + nz // 2, nz - nz // 2)

    def over(x_lo, x_hi, nx, z_lo, z_hi, body):
        def at(i, _):
            body(x_lo + i * nx, nx, z_lo, z_hi - z_lo)
            return 0

        lax.fori_loop(0, (x_hi - x_lo) // nx, at, 0)

    def set_coefficients(x, nx, z0, nz):
        xs, zs = pl.ds(x, nx), pl.ds(z0, nz)
        s, a, b = coefficients(sigma[xs, zs], tags[xs, zs])
        sigma[xs, zs] = s
        ca[xs, zs] = a
        cb[xs, zs] = b
        for i in range(nx):
            power[power_rows(x + i, z0, nz)] = jnp.zeros((nz * 8, 128), F32)

    def corrections(t):
        @pl.when(has_cp)
        def _():
            h[1, sx, pl.ds(1, sz)] = h[1, sx, pl.ds(1, sz)] + COURANT * xp[t, 1]
            h[2, sx, pl.ds(1, sz)] = h[2, sx, pl.ds(1, sz)] - COURANT * xp[t, 0]

        @pl.when(has_cm)
        def _():
            h[1, 0, pl.ds(1, sz)] = xm[t, 0] + COURANT * e[2, 0, pl.ds(0, sz)]
            h[2, 0, pl.ds(1, sz)] = xm[t, 1] - COURANT * e[1, 0, pl.ds(0, sz)]

        @pl.when(has_cm & has_hp)
        def _():
            h[1, 0, sz] = h[1, 0, sz] - COURANT * cm[t]

        planes, own = pl.ds(1, sx), pl.ds(0, sx)

        @pl.when(has_hp)
        def _():
            h[0, planes, sz] = h[0, planes, sz] + COURANT * zp[t, 1]
            h[1, planes, sz] = h[1, planes, sz] - COURANT * zp[t, 0]

        @pl.when(has_hm)
        def _():
            h[0, planes, 0] = zm[t, 0] + COURANT * e[1, own, 0]
            h[1, planes, 0] = zm[t, 1] - COURANT * e[0, own, 0]

        @pl.when(has_cp & has_hm)
        def _():
            h[1, sx, 0] = h[1, sx, 0] + COURANT * cp[t]

    me = c * nh + g

    def partner(d):
        t = me ^ ((d * 11) % n_dev)
        return t, (t // nh, t % nh)

    def node_copy(d):
        t, device = partner(d)
        return pltpu.make_async_remote_copy(
            src_ref=nodes.at[t], dst_ref=recv_nodes.at[d], send_sem=node_out_sem, recv_sem=node_in_sem,
            device_id=device, device_id_type=MESH)

    def send_nodes(d, _):
        node_copy(d).start()
        return 0

    def block_copy(d):
        device = partner(d)[1]
        return pltpu.make_async_remote_copy(
            src_ref=send.at[d], dst_ref=recv.at[d], send_sem=out_sem,
            recv_sem=in_sem.at[d // GROUP], device_id=device, device_id_type=MESH)

    def gather(d):
        t = partner(d)[0]
        for r in range(cap):
            i = jnp.clip(source[t, r], 0, sx * sz * 8 - 1)
            send[d, pl.ds(r, 1)] = power[pl.ds(i, 1)]

    route(n_dev, cap, owner, node, source_vmem, nodes)
    for w in range(6, 8):
        for copy in all_loads[w]:
            copy.wait()
    over(0, sx, 1, 0, sz, set_coefficients)
    to_smem = pltpu.make_async_copy(source_vmem, source, local_sem.at[2])
    to_smem.start()
    to_smem.wait()
    pl.semaphore_wait(barrier, peers)
    along_col(ready)
    for w in range(6):
        for copy in all_loads[w]:
            copy.wait()
    for t in range(STEPS):
        update_h(sx - 1, 1, 0, sz)
        update_h(0, sx - 1, sz - 1, 1)
        for sends, _, copy in copies(t):
            pl.when(sends)(copy.start)
        over(0, sx - 1, planes_h, 0, sz - 1, update_h)
        over(1, sx - 1, 1, 1, sz - 1, update_e_in_halves)
        if t == 1:
            pl.semaphore_wait(ready, nc - 1)
            own_nodes = pltpu.make_async_copy(nodes.at[me], recv_nodes.at[0], local_sem.at[0])
            own_nodes.start()
            lax.fori_loop(1, n_dev, send_nodes, 0)
        for sends, receives, copy in copies(t):
            pl.when(sends)(copy.wait_send)
            pl.when(receives)(copy.wait_recv)
        corrections(t)
        update_e(0, 1, 0, sz)
        update_e(sx - 1, 1, 0, sz)
        update_e(1, sx - 2, 0, 1)
        update_e(1, sx - 2, sz - 1, 1)

    gather(0)
    gather(1)
    own = pltpu.make_async_copy(send.at[0], recv.at[0], local_sem.at[1])
    own.start()

    def exchange(d, _):
        gather(d)
        block_copy(d - 1).start()
        return 0

    lax.fori_loop(2, n_dev, exchange, 0)
    own.wait()
    own_nodes.wait()
    block_copy(n_dev - 1).start()
    others = pl.ds(0, n_dev - 1)
    pltpu.make_async_copy(recv_nodes.at[others], recv_nodes.at[others], node_in_sem).wait()
    pltpu.make_async_copy(recv_nodes.at[others], recv_nodes.at[others], node_out_sem).wait()

    n_nodes = heat_out.shape[0]
    span = GROUP * cap
    count = lax.broadcasted_iota(jnp.int32, (n_nodes, span), 0).astype(F32) + 1.0

    def deposit(i, heat):
        tag = jnp.concatenate([recv_nodes[i * GROUP + j][:, :cap] for j in range(GROUP)], axis=1)
        pick = jnp.where(count == tag, 1.0, 0.0).astype(jnp.bfloat16)
        blocks = recv[pl.ds(i * GROUP, GROUP)].reshape(span, 128)
        high = blocks.astype(jnp.bfloat16)
        low = (blocks - high.astype(F32)).astype(jnp.bfloat16)
        both = jnp.dot(pick, jnp.concatenate([high, low], axis=1), preferred_element_type=F32)
        return heat + (both[:, :128] + both[:, 128:])

    def arrived(i, n):
        part = recv.at[pl.ds(0, n)]
        pltpu.make_async_copy(part, part, in_sem.at[i]).wait()

    def collect(i, heat):
        arrived(i, GROUP)
        return deposit(i, heat)

    arrived(0, GROUP - 1)
    heat = deposit(0, jnp.zeros((n_nodes, 128), F32))
    heat = lax.fori_loop(1, n_dev // GROUP, collect, heat)
    heat_out[...] = heat
    pltpu.make_async_copy(recv.at[others], recv.at[others], out_sem).wait()


def store_kernel(e, h, heat, enthalpy, e_hbm, h_hbm, temp, sem):
    sx, sz = e_hbm.shape[1], e_hbm.shape[2]
    copies = []
    for i in range(3):
        for k in range(e_hbm.shape[3] // 128):
            copies.append(pltpu.make_async_copy(
                e.at[i, pl.ds(0, sx), pl.ds(0, sz), k, :], e_hbm.at[i, :, :, pl.ds(k * 128, 128)], sem))
            copies.append(pltpu.make_async_copy(
                h.at[i, pl.ds(1, sx), pl.ds(1, sz), k, :], h_hbm.at[i, :, :, pl.ds(k * 128, 128)], sem))
    for copy in copies:
        copy.start()
    q = enthalpy[...] + (0.25 / STEPS) * heat[...]
    temp[...] = jnp.where(q < 0.0, q / 2.0, jnp.where(q > 1.0, (q - 1.0) / 3.0, 0.0))
    for copy in copies:
        copy.wait()


def per_device(nc, nh, efield, hfield, cell_temp, region_tags, block_owner, block_node, node_enthalpy):
    sx, sz, sy = cell_temp.shape
    n_dev = nc * nh
    blocks = sx * sz * sy // 128
    cap = 2 * blocks // n_dev
    dma = pltpu.SemaphoreType.DMA

    def tiles(*shape):
        return pltpu.VMEM(shape + (8, 128), F32)

    def out(*shape):
        return jax.ShapeDtypeStruct(shape, F32)

    def native(table):
        return table.reshape(sx, sz, sy // 128).transpose(0, 2, 1)

    e, h, heat = pl.pallas_call(
        lambda *refs: fields_kernel(nc, nh, cap, *refs),
        out_shape=(tiles(3, sx + 1, sz + 1), tiles(3, sx + 1, sz + 1), pltpu.VMEM(node_enthalpy.shape, F32)),
        in_specs=[HBM] * 4 + [VMEM, VMEM],
        out_specs=(VMEM, VMEM, VMEM),
        scratch_shapes=[
            pltpu.VMEM((n_dev, 128), jnp.int32), pltpu.SMEM((n_dev, 128), jnp.int32), pltpu.VMEM((n_dev, 1, 128), F32),
            pltpu.VMEM((sx * sz * 8, 128), F32), pltpu.VMEM((sx, sz, 8, 128), jnp.int32), tiles(sx, sz), tiles(sx, sz), tiles(sx, sz),
            tiles(STEPS, 2, sz), tiles(STEPS, 2, sx), tiles(STEPS, 2, sz), tiles(STEPS, 2, sx), tiles(STEPS), tiles(STEPS),
            pltpu.VMEM((n_dev, cap, 128), F32), pltpu.VMEM((n_dev, cap, 128), F32), pltpu.VMEM((n_dev, 1, 128), F32),
            dma((8,)), dma((STEPS, 6)), dma((STEPS, 6)), pltpu.SemaphoreType.REGULAR, dma((3,)), dma, dma((n_dev // GROUP,)), dma, dma,
        ],
        compiler_params=pltpu.CompilerParams(collective_id=0, has_side_effects=True, vmem_limit_bytes=48 << 20),
        name="fields",
    )(efield, hfield, cell_temp, region_tags, native(block_owner), native(block_node))
    return pl.pallas_call(
        store_kernel,
        out_shape=(out(3, sx, sz, sy), out(3, sx, sz, sy), out(*node_enthalpy.shape)),
        in_specs=[VMEM] * 4,
        out_specs=(HBM, HBM, VMEM),
        scratch_shapes=[dma],
        compiler_params=pltpu.CompilerParams(vmem_limit_bytes=24 << 20),
        name="store",
    )(e, h, heat, node_enthalpy)


def solution(mesh):
    placed = (
        P(None, "col", "hgt", None),
        P(None, "col", "hgt", None),
        P("col", "hgt", None),
        P("col", "hgt", None),
        P("col", "hgt", None, None, None, None),
        P("col", "hgt", None, None, None),
        P(("col", "hgt"), None),
    )
    nc, nh = mesh.shape["col"], mesh.shape["hgt"]
    return jax.shard_map(
        lambda *args: per_device(nc, nh, *args),
        mesh=mesh,
        in_specs=placed,
        out_specs=(P(None, "col", "hgt", None), P(None, "col", "hgt", None), P(("col", "hgt"), None)),
        check_vma=False,
    )
```

```python
import jax
import jax.numpy as jnp
from jax import lax
from jax.experimental import pallas as pl
from jax.experimental.pallas import tpu as pltpu
from jax.sharding import PartitionSpec as P

STEPS = 4
COURANT = 0.55
GROUP = 8
MESH = pl.DeviceIdType.MESH
F32 = jnp.float32
HBM = pl.BlockSpec(memory_space=pltpu.HBM)
VMEM = pl.BlockSpec(memory_space=pltpu.VMEM)


def shifted_up(f):
    axis = f.ndim - 1
    lane = lax.broadcasted_iota(jnp.int32, f.shape, axis)
    sub = lax.broadcasted_iota(jnp.int32, f.shape, axis - 1)
    r = pltpu.roll(f, 127, axis)
    u = pltpu.roll(r, 7, axis - 1)
    return jnp.where(lane < 127, r, jnp.where(sub < 7, u, 0.0))


def shifted_down(f):
    axis = f.ndim - 1
    lane = lax.broadcasted_iota(jnp.int32, f.shape, axis)
    sub = lax.broadcasted_iota(jnp.int32, f.shape, axis - 1)
    r = pltpu.roll(f, 1, axis)
    u = pltpu.roll(r, 1, axis - 1)
    return jnp.where(lane > 0, r, jnp.where(sub > 0, u, 0.0))


def coefficients(temp, tags):
    frac = 1.0 / (1.0 + jnp.exp(-2.0 * temp))
    lean = tags == 0
    fat = tags == 1
    eps_frozen = jnp.where(lean, 4.0, jnp.where(fat, 2.5, 5.0))
    eps_span = jnp.where(lean, 46.0, jnp.where(fat, 3.5, 5.0))
    sig_frozen = jnp.where(lean, 0.2, jnp.where(fat, 0.05, 0.1))
    sig_span = jnp.where(lean, 7.8, jnp.where(fat, 0.35, 0.9))
    eps2 = 2.0 * (eps_frozen + eps_span * frac)
    sigma = sig_frozen + sig_span * frac
    half = sigma * COURANT
    inv = 1.0 / (eps2 + half)
    return sigma, (eps2 - half) * inv, (2.0 * COURANT) * inv


def route(n_dev, cap, owner_ref, node_ref, source_ref, nodes_ref):
    sx, nk, sz = owner_ref.shape
    per = max(p for p in range(1, 128 // sz + 1) if sx % p == 0)
    who = lax.broadcasted_iota(jnp.int32, (n_dev, 128), 0)
    earlier = (lax.broadcasted_iota(jnp.int32, (128, 128), 0) < lax.broadcasted_iota(jnp.int32, (128, 128), 1)).astype(jnp.bfloat16)
    slot = lax.broadcasted_iota(jnp.int32, (cap, 128), 0)
    lane = lax.broadcasted_iota(jnp.int32, (1, 128), 1).astype(F32)
    first = lax.broadcasted_iota(jnp.int32, (1, 4 * cap), 1) < cap
    base = jnp.zeros((n_dev, 1), F32)
    sums = jnp.zeros((n_dev, 4 * cap), F32)
    for q in range(sx // per):
        fill = jnp.full((nk, 128 - per * sz), -1, jnp.int32)
        owners = jnp.concatenate([owner_ref[q * per + i] for i in range(per)] + [fill], axis=1)
        tags = jnp.concatenate([node_ref[q * per + i] for i in range(per)] + [fill], axis=1) + 1
        tags_hi = (tags // 16).astype(F32)
        tags_lo = (tags % 16).astype(F32)
        for k in range(nk):
            hit = who == owners[k : k + 1]
            hit_f = hit.astype(F32)
            hit_b = hit_f.astype(jnp.bfloat16)
            before = jnp.dot(hit_b, earlier, preferred_element_type=F32) + base
            rank = jnp.sum(hit_f * before, axis=0, keepdims=True).astype(jnp.int32)
            base = base + jnp.sum(hit_f, axis=1, keepdims=True)
            at = slot == rank
            values = (1.0, lane, tags_hi[k : k + 1], tags_lo[k : k + 1])
            table = jnp.concatenate([jnp.where(at, value, 0.0) for value in values], axis=0).astype(jnp.bfloat16)
            got = lax.dot_general(hit_b, table, (((1,), (1,)), ((), ())), preferred_element_type=F32)
            sums = sums + got * jnp.where(first, float(q * per * sz * nk + k), 1.0)
    source_ref[:, :cap] = (sums[:, :cap] + float(nk) * sums[:, cap : 2 * cap]).astype(jnp.int32)
    tag = 16.0 * sums[:, 2 * cap : 3 * cap] + sums[:, 3 * cap :]
    nodes_ref[...] = jnp.concatenate([tag, jnp.zeros((n_dev, 128 - cap), F32)], axis=1).reshape(n_dev, 1, 128)


def fields_kernel(nc, nh, cap, e_hbm, h_hbm, t_hbm, g_hbm, owner, node, e, h, heat_out,
                  source_vmem, source, nodes, power, tags, sigma, ca, cb, xp, zp, xm, zm, cm, cp, send, recv, recv_nodes,
                  load_sem, ssem, rsem, ready, local_sem, out_sem, in_sem, node_out_sem, node_in_sem):
    n_dev = nc * nh
    sx, sz = t_hbm.shape[0], t_hbm.shape[1]
    nk = t_hbm.shape[2] // 128
    c = lax.axis_index("col")
    g = lax.axis_index("hgt")
    planes_h = max(p for p in (1, 2, 3) if (sx - 1) % p == 0)
    has_cp, has_cm = c < nc - 1, c > 0
    has_hp, has_hm = g < nh - 1, g > 0

    def lanes(k):
        return pl.ds(k * 128, 128)

    def loads(which):
        out = []
        for k in range(nk):
            if which < 3:
                out.append(pltpu.make_async_copy(
                    e_hbm.at[which, :, :, lanes(k)], e.at[which, pl.ds(0, sx), pl.ds(0, sz), k, :], load_sem.at[which]))
            elif which < 6:
                out.append(pltpu.make_async_copy(
                    h_hbm.at[which - 3, :, :, lanes(k)], h.at[which - 3, pl.ds(1, sx), pl.ds(1, sz), k, :], load_sem.at[which]))
            elif which == 6:
                out.append(pltpu.make_async_copy(t_hbm.at[:, :, lanes(k)], sigma.at[:, :, k, :], load_sem.at[which]))
            else:
                out.append(pltpu.make_async_copy(g_hbm.at[:, :, lanes(k)], tags.at[:, :, k, :], load_sem.at[which]))
        return out

    all_loads = [loads(w) for w in range(8)]
    for w in (6, 7, 0, 1, 2, 3, 4, 5):
        for copy in all_loads[w]:
            copy.start()

    plan = [
        (has_cm, (c - 1, g), has_cp, e.at[pl.ds(1, 2), 0, pl.ds(0, sz)], xp),
        (has_hm, (c, g - 1), has_hp, e.at[pl.ds(0, 2), pl.ds(0, sx), 0], zp),
        (has_cp, (c + 1, g), has_cm, h.at[pl.ds(1, 2), sx, pl.ds(1, sz)], xm),
        (has_hp, (c, g + 1), has_hm, h.at[pl.ds(0, 2), pl.ds(1, sx), sz], zm),
        (has_cp & has_hm, (c + 1, g - 1), has_cm & has_hp, e.at[0, sx - 1, 0], cm),
        (has_cm & has_hp, (c - 1, g + 1), has_cp & has_hm, e.at[2, 0, sz - 1], cp),
    ]

    barrier = pltpu.get_barrier_semaphore()

    def greet(semaphore, device):
        pl.semaphore_signal(semaphore, inc=1, device_id=device, device_id_type=MESH)

    def along_col(semaphore):
        def one(i, _):
            greet(semaphore, (lax.rem(c + i, nc), g))
            return 0

        lax.fori_loop(1, nc, one, 0)

    def along_hgt(i, _):
        greet(barrier, (c, lax.rem(g + i, nh)))
        return 0

    lax.fori_loop(1, nh, along_hgt, 0)
    along_col(barrier)
    peers = nc + nh - 2
    for sends, device, _, _, _ in plan[4:]:
        @pl.when(sends)
        def _(device=device):
            greet(barrier, device)
        peers = peers + sends.astype(jnp.int32)
    zero_tile = jnp.zeros((8, 128), F32)
    for i in range(3):
        e[i, sx] = jnp.zeros((sz + 1, 8, 128), F32)
        h[i, 0] = jnp.zeros((sz + 1, 8, 128), F32)

    def clear(x, _):
        for i in range(3):
            e[i, x, sz] = zero_tile
            h[i, x + 1, 0] = zero_tile
        return 0

    lax.fori_loop(0, sx, clear, 0)
    def copies(t):
        out = []
        for j, (sends, device, receives, src, buf) in enumerate(plan):
            out.append((sends, receives, pltpu.make_async_remote_copy(
                src_ref=src, dst_ref=buf.at[t], send_sem=ssem.at[t, j], recv_sem=rsem.at[t, j],
                device_id=device, device_id_type=MESH)))
        return out

    def update_h(x, nx, z0, nz):
        xs, xn, zs, zn, zw = pl.ds(x, nx), pl.ds(x + 1, nx), pl.ds(z0, nz), pl.ds(z0 + 1, nz), pl.ds(z0, nz + 1)
        ex, ey, ez = e[0, xs, zw], e[1, xs, zw], e[2, xs, zs]
        ey_x, ez_x = e[1, xn, zs], e[2, xn, zs]
        hx, hy, hz = h[0, xn, zn], h[1, xn, zn], h[2, xn, zn]
        ex, ex_z = ex[:, :nz], ex[:, 1:]
        ey, ey_z = ey[:, :nz], ey[:, 1:]
        hx = hx - COURANT * ((shifted_up(ez) - ez) - (ey_z - ey))
        hy = hy - COURANT * ((ex_z - ex) - (ez_x - ez))
        hz = hz - COURANT * ((ey_x - ey) - (shifted_up(ex) - ex))
        h[0, xn, zn] = hx
        h[1, xn, zn] = hy
        h[2, xn, zn] = hz

    def power_rows(x, z0, nz):
        return pl.ds(pl.multiple_of((x * sz + z0) * 8, 8), nz * 8)

    def update_e(x, nx, z0, nz):
        xs, xn, zs, zn, zw = pl.ds(x, nx), pl.ds(x + 1, nx), pl.ds(z0, nz), pl.ds(z0 + 1, nz), pl.ds(z0, nz + 1)
        hx, hy, hz = h[0, xn, zw], h[1, xn, zw], h[2, xn, zn]
        hy_x, hz_x = h[1, xs, zn], h[2, xs, zn]
        ex, ey, ez = e[0, xs, zs], e[1, xs, zs], e[2, xs, zs]
        a, b, s = ca[xs, zs], cb[xs, zs], sigma[xs, zs]
        lines = [power_rows(x + i, z0, nz) for i in range(nx)]
        p = [power[line].reshape(nz, 8, 128) for line in lines]
        hx_z, hx = hx[:, :nz], hx[:, 1:]
        hy_z, hy = hy[:, :nz], hy[:, 1:]
        ex = a * ex + b * ((hz - shifted_down(hz)) - (hy - hy_z))
        ey = a * ey + b * ((hx - hx_z) - (hz - hz_x))
        ez = a * ez + b * ((hy - hy_x) - (hx - shifted_down(hx)))
        e[0, xs, zs] = ex
        e[1, xs, zs] = ey
        e[2, xs, zs] = ez
        dissipated = s * (ex * ex + ey * ey + ez * ez)
        for i in range(nx):
            power[lines[i]] = (p[i] + dissipated[i]).reshape(nz * 8, 128)

    def update_e_in_halves(x, nx, z0, nz):
        update_e(x, nx, z0, nz // 2)
        update_e(x, nx, z0 + nz // 2, nz - nz // 2)

    def over(x_lo, x_hi, nx, z_lo, z_hi, body):
        def at(i, _):
            body(x_lo + i * nx, nx, z_lo, z_hi - z_lo)
            return 0

        lax.fori_loop(0, (x_hi - x_lo) // nx, at, 0)

    def set_coefficients(x, nx, z0, nz):
        xs, zs = pl.ds(x, nx), pl.ds(z0, nz)
        s, a, b = coefficients(sigma[xs, zs], tags[xs, zs])
        sigma[xs, zs] = s
        ca[xs, zs] = a
        cb[xs, zs] = b
        for i in range(nx):
            power[power_rows(x + i, z0, nz)] = jnp.zeros((nz * 8, 128), F32)

    def corrections(t):
        @pl.when(has_cp)
        def _():
            h[1, sx, pl.ds(1, sz)] = h[1, sx, pl.ds(1, sz)] + COURANT * xp[t, 1]
            h[2, sx, pl.ds(1, sz)] = h[2, sx, pl.ds(1, sz)] - COURANT * xp[t, 0]

        @pl.when(has_cm)
        def _():
            h[1, 0, pl.ds(1, sz)] = xm[t, 0] + COURANT * e[2, 0, pl.ds(0, sz)]
            h[2, 0, pl.ds(1, sz)] = xm[t, 1] - COURANT * e[1, 0, pl.ds(0, sz)]

        @pl.when(has_cm & has_hp)
        def _():
            h[1, 0, sz] = h[1, 0, sz] - COURANT * cm[t]

        planes, own = pl.ds(1, sx), pl.ds(0, sx)

        @pl.when(has_hp)
        def _():
            h[0, planes, sz] = h[0, planes, sz] + COURANT * zp[t, 1]
            h[1, planes, sz] = h[1, planes, sz] - COURANT * zp[t, 0]

        @pl.when(has_hm)
        def _():
            h[0, planes, 0] = zm[t, 0] + COURANT * e[1, own, 0]
            h[1, planes, 0] = zm[t, 1] - COURANT * e[0, own, 0]

        @pl.when(has_cp & has_hm)
        def _():
            h[1, sx, 0] = h[1, sx, 0] + COURANT * cp[t]

    me = c * nh + g

    def partner(d):
        t = me ^ ((d * 11) % n_dev)
        return t, (t // nh, t % nh)

    def node_copy(d):
        t, device = partner(d)
        return pltpu.make_async_remote_copy(
            src_ref=nodes.at[t], dst_ref=recv_nodes.at[d], send_sem=node_out_sem, recv_sem=node_in_sem,
            device_id=device, device_id_type=MESH)

    def send_nodes(d, _):
        node_copy(d).start()
        return 0

    def block_copy(d):
        device = partner(d)[1]
        return pltpu.make_async_remote_copy(
            src_ref=send.at[d], dst_ref=recv.at[d], send_sem=out_sem,
            recv_sem=in_sem.at[d // GROUP], device_id=device, device_id_type=MESH)

    def gather(d):
        t = partner(d)[0]
        for r in range(cap):
            i = jnp.clip(source[t, r], 0, sx * sz * 8 - 1)
            send[d, pl.ds(r, 1)] = power[pl.ds(i, 1)]

    route(n_dev, cap, owner, node, source_vmem, nodes)
    for w in range(6, 8):
        for copy in all_loads[w]:
            copy.wait()
    over(0, sx, 1, 0, sz, set_coefficients)
    to_smem = pltpu.make_async_copy(source_vmem, source, local_sem.at[2])
    to_smem.start()
    to_smem.wait()
    pl.semaphore_wait(barrier, peers)
    along_col(ready)
    def start(t, which):
        group = copies(t)
        for j in which:
            pl.when(group[j][0])(group[j][2].start)

    for w in range(3):
        for copy in all_loads[w]:
            copy.wait()
    start(0, (0, 1))
    for w in range(3, 6):
        for copy in all_loads[w]:
            copy.wait()
    for t in range(STEPS):
        update_h(sx - 1, 1, 0, sz)
        if t > 0:
            start(t, (0, 1))
        update_h(0, sx - 1, sz - 1, 1)
        start(t, (4, 5, 2, 3))
        over(0, sx - 1, planes_h, 0, sz - 1, update_h)
        over(1, sx - 1, 1, 1, sz - 1, update_e_in_halves)
        if t == 1:
            pl.semaphore_wait(ready, nc - 1)
            own_nodes = pltpu.make_async_copy(nodes.at[me], recv_nodes.at[0], local_sem.at[0])
            own_nodes.start()
            lax.fori_loop(1, n_dev, send_nodes, 0)
        for sends, receives, copy in copies(t):
            pl.when(sends)(copy.wait_send)
            pl.when(receives)(copy.wait_recv)
        corrections(t)
        update_e(0, 1, 0, sz)
        update_e(sx - 1, 1, 0, sz)
        update_e(1, sx - 2, 0, 1)
        update_e(1, sx - 2, sz - 1, 1)

    gather(0)
    gather(1)
    own = pltpu.make_async_copy(send.at[0], recv.at[0], local_sem.at[1])
    own.start()

    def exchange(d, _):
        gather(d)
        block_copy(d - 1).start()
        return 0

    lax.fori_loop(2, n_dev, exchange, 0)
    own.wait()
    own_nodes.wait()
    block_copy(n_dev - 1).start()
    others = pl.ds(0, n_dev - 1)
    pltpu.make_async_copy(recv_nodes.at[others], recv_nodes.at[others], node_in_sem).wait()
    pltpu.make_async_copy(recv_nodes.at[others], recv_nodes.at[others], node_out_sem).wait()

    n_nodes = heat_out.shape[0]
    span = GROUP * cap
    count = lax.broadcasted_iota(jnp.int32, (n_nodes, span), 0).astype(F32) + 1.0

    def deposit(i, heat):
        tag = jnp.concatenate([recv_nodes[i * GROUP + j][:, :cap] for j in range(GROUP)], axis=1)
        pick = jnp.where(count == tag, 1.0, 0.0).astype(jnp.bfloat16)
        blocks = recv[pl.ds(i * GROUP, GROUP)].reshape(span, 128)
        high = blocks.astype(jnp.bfloat16)
        low = (blocks - high.astype(F32)).astype(jnp.bfloat16)
        both = jnp.dot(pick, jnp.concatenate([high, low], axis=1), preferred_element_type=F32)
        return heat + (both[:, :128] + both[:, 128:])

    def arrived(i, n):
        part = recv.at[pl.ds(0, n)]
        pltpu.make_async_copy(part, part, in_sem.at[i]).wait()

    def collect(i, heat):
        arrived(i, GROUP)
        return deposit(i, heat)

    arrived(0, GROUP - 1)
    heat = deposit(0, jnp.zeros((n_nodes, 128), F32))
    heat = lax.fori_loop(1, n_dev // GROUP, collect, heat)
    heat_out[...] = heat
    pltpu.make_async_copy(recv.at[others], recv.at[others], out_sem).wait()


def store_kernel(e, h, heat, enthalpy, e_hbm, h_hbm, temp, sem):
    sx, sz = e_hbm.shape[1], e_hbm.shape[2]
    copies = []
    for i in range(3):
        for k in range(e_hbm.shape[3] // 128):
            copies.append(pltpu.make_async_copy(
                e.at[i, pl.ds(0, sx), pl.ds(0, sz), k, :], e_hbm.at[i, :, :, pl.ds(k * 128, 128)], sem))
            copies.append(pltpu.make_async_copy(
                h.at[i, pl.ds(1, sx), pl.ds(1, sz), k, :], h_hbm.at[i, :, :, pl.ds(k * 128, 128)], sem))
    for copy in copies:
        copy.start()
    q = enthalpy[...] + (0.25 / STEPS) * heat[...]
    temp[...] = jnp.where(q < 0.0, q / 2.0, jnp.where(q > 1.0, (q - 1.0) / 3.0, 0.0))
    for copy in copies:
        copy.wait()


def per_device(nc, nh, efield, hfield, cell_temp, region_tags, block_owner, block_node, node_enthalpy):
    sx, sz, sy = cell_temp.shape
    n_dev = nc * nh
    blocks = sx * sz * sy // 128
    cap = 2 * blocks // n_dev
    dma = pltpu.SemaphoreType.DMA

    def tiles(*shape):
        return pltpu.VMEM(shape + (8, 128), F32)

    def out(*shape):
        return jax.ShapeDtypeStruct(shape, F32)

    def native(table):
        return table.reshape(sx, sz, sy // 128).transpose(0, 2, 1)

    e, h, heat = pl.pallas_call(
        lambda *refs: fields_kernel(nc, nh, cap, *refs),
        out_shape=(tiles(3, sx + 1, sz + 1), tiles(3, sx + 1, sz + 1), pltpu.VMEM(node_enthalpy.shape, F32)),
        in_specs=[HBM] * 4 + [VMEM, VMEM],
        out_specs=(VMEM, VMEM, VMEM),
        scratch_shapes=[
            pltpu.VMEM((n_dev, 128), jnp.int32), pltpu.SMEM((n_dev, 128), jnp.int32), pltpu.VMEM((n_dev, 1, 128), F32),
            pltpu.VMEM((sx * sz * 8, 128), F32), pltpu.VMEM((sx, sz, 8, 128), jnp.int32), tiles(sx, sz), tiles(sx, sz), tiles(sx, sz),
            tiles(STEPS, 2, sz), tiles(STEPS, 2, sx), tiles(STEPS, 2, sz), tiles(STEPS, 2, sx), tiles(STEPS), tiles(STEPS),
            pltpu.VMEM((n_dev, cap, 128), F32), pltpu.VMEM((n_dev, cap, 128), F32), pltpu.VMEM((n_dev, 1, 128), F32),
            dma((8,)), dma((STEPS, 6)), dma((STEPS, 6)), pltpu.SemaphoreType.REGULAR, dma((3,)), dma, dma((n_dev // GROUP,)), dma, dma,
        ],
        compiler_params=pltpu.CompilerParams(collective_id=0, has_side_effects=True, vmem_limit_bytes=48 << 20),
        name="fields",
    )(efield, hfield, cell_temp, region_tags, native(block_owner), native(block_node))
    return pl.pallas_call(
        store_kernel,
        out_shape=(out(3, sx, sz, sy), out(3, sx, sz, sy), out(*node_enthalpy.shape)),
        in_specs=[VMEM] * 4,
        out_specs=(HBM, HBM, VMEM),
        scratch_shapes=[dma],
        compiler_params=pltpu.CompilerParams(vmem_limit_bytes=24 << 20),
        name="store",
    )(e, h, heat, node_enthalpy)


def solution(mesh):
    placed = (
        P(None, "col", "hgt", None),
        P(None, "col", "hgt", None),
        P("col", "hgt", None),
        P("col", "hgt", None),
        P("col", "hgt", None, None, None, None),
        P("col", "hgt", None, None, None),
        P(("col", "hgt"), None),
    )
    nc, nh = mesh.shape["col"], mesh.shape["hgt"]
    return jax.shard_map(
        lambda *args: per_device(nc, nh, *args),
        mesh=mesh,
        in_specs=placed,
        out_specs=(P(None, "col", "hgt", None), P(None, "col", "hgt", None), P(("col", "hgt"), None)),
        check_vma=False,
    )
```
